32 devices in a mesh: mod: 2 (over core), ctx: 4 (over z), dp: 4 (over y, x).
Axes of the slice: x: 2, y: 2, z: 4, core: 2. Of those that a mesh axis runs over, the one named last changes fastest.
Arguments:
- hidden_in: bfloat16 [4, 64, 4096], P('dp', ('mod', 'ctx')), may hold values from -6 to 6
- query_modality: int32 [4, 64], P('dp', ('mod', 'ctx')), may hold values from 0 to 1, as said below
- key_cache: bfloat16 [4, 8192, 4096], P('dp', None, 'ctx'), may hold values from -6 to 6
- value_cache: bfloat16 [4, 8192, 4096], P('dp', None, 'ctx'), may hold values from -6 to 6
- key_modality: int32 [4, 8192], P('dp'), may hold values from 0 to 1
- norm_attn: float32 [2, 4096], P('mod'), may hold values from 0.5 to 1.5
- query_weight: bfloat16 [2, 4096, 4096], P('mod', 'dp', 'ctx'), may hold values from -0.09375 to 0.09375
- query_gain: float32 [2, 4096], P('mod', 'ctx'), may hold values from 0.5 to 2.5
- key_gain: float32 [2, 4096], P(None, 'ctx'), may hold values from 0.5 to 2.5
- out_weight: bfloat16 [2, 4096, 4096], P('mod', 'ctx', 'dp'), may hold values from -0.09375 to 0.09375
- norm_ffn: float32 [2, 4096], P('mod'), may hold values from 0.5 to 1.5
- gate_weight: bfloat16 [2, 4096, 11008], P('mod', 'dp', 'ctx'), may hold values from -0.09375 to 0.09375
- up_weight: bfloat16 [2, 4096, 11008], P('mod', 'dp', 'ctx'), may hold values from -0.09375 to 0.09375
- down_weight: bfloat16 [2, 11008, 4096], P('mod', 'ctx', 'dp'), may hold values from -0.0546875 to 0.0546875
Outputs:
- mixed_out: bfloat16 [4, 64, 4096], P('dp', ('mod', 'ctx'))
The draws below stay inside these ranges and needn't reach their ends.
Inputs may be any that keep to these rules, and one draw needn't show every extreme that they name: `query_modality`: each sequence has one main modality, drawn. The slab splits into aligned blocks of 8 tokens, one block a device; in each aligned pair of blocks (2j and 2j + 1) one block holds 6 tokens of the main modality and the other 4, the rest being the other modality, so a sequence's slab holds exactly 40 tokens of its main modality.
All inputs are finite; a program needn't handle non-finite values.
Results may differ from the reference program's by a relative error of at most 0.007.
Values may be sent and summed in bfloat16 or wider, within the bound.
A program may use at most 320 MiB of HBM per device.

```python
import math
import jax
import jax.numpy as jnp
from jax import lax

D = 4096
HEADS = 32
FF = 11008
HD = 128
ROWS_DEV = 8
CACHE = 8192
SEQS = 4
SLAB = 64
LCAP = 6
LOW = 4
MAIN = 40


def draw_query_modality(key, part):
    blocks = SLAB // ROWS_DEV
    key_main, key_flip, key_perm = jax.random.split(key, 3)
    main_mod = jax.random.randint(key_main, (SEQS, 1, 1), 0, 2)
    pair_flips = jax.random.randint(key_flip, (SEQS, blocks // 2, 1), 0, 2)
    first_count = jnp.where(pair_flips == 1, LCAP, LOW)
    counts = jnp.concatenate([first_count, LCAP + LOW - first_count], axis=2).reshape(SEQS, blocks, 1)
    perm_keys = jax.random.split(key_perm, SEQS * blocks)
    row_perms = jax.vmap(lambda one_key: jax.random.permutation(one_key, ROWS_DEV))(perm_keys).reshape(SEQS, blocks, ROWS_DEV)
    is_main = row_perms < counts
    modality_ids = jnp.where(is_main, main_mod, 1 - main_mod)
    return modality_ids.reshape(SEQS, SLAB).astype(jnp.int32)


def set_ends(entries, rng, smallest, top_value):
    longest = entries.shape.index(max(entries.shape))
    spots = []
    for shift in (0, 1):
        where = [jax.random.randint(jax.random.fold_in(rng, axis), (), 0, length) for axis, length in enumerate(entries.shape)]
        where[longest] = (where[longest] + shift) % entries.shape[longest]
        spots.append(tuple(where))
    return entries.at[spots[0]].set(smallest).at[spots[1]].set(top_value)


def block_scale(key, dims, shards, low, largest):
    def one(dim, parts):
        draws = jax.random.uniform(jax.random.fold_in(jax.random.fold_in(key, 6), dim), (parts,), jnp.float32, low / len(shards), largest / len(shards))
        return jnp.repeat(jnp.exp(draws), dims[dim] // parts).reshape((-1,) + (1,) * (len(dims) - dim - 1))

    gain = one(*shards[0])
    for cut in shards[1:]:
        gain = gain * one(*cut)
    return gain


def gaussian(own_key, shape, width, reach, cuts=(), kind=jnp.bfloat16):
    values = jax.random.normal(own_key, shape, jnp.float32) * width
    if len(cuts) > 0:
        values = block_scale(own_key, shape, cuts, -0.22, 0.18) * values
    return jnp.clip(values, min=-reach, max=reach).astype(kind)


def setup_inputs(seed: int = 0) -> dict:
    key_of = jax.random.split(jax.random.key(seed), 15)
    return {
        "hidden_in": gaussian(key_of[0], (SEQS, SLAB, D), 1.0, 6.0, ((0, 4), (1, 8))),
        "query_modality": draw_query_modality(jax.random.fold_in(key_of[14], 71), 0),
        "key_cache": gaussian(key_of[2], (SEQS, CACHE, D), 1.0, 6.0, ((0, 4), (2, 4))),
        "value_cache": gaussian(key_of[3], (SEQS, CACHE, D), 1.0, 6.0, ((0, 4), (2, 4))),
        "key_modality": set_ends(jax.random.randint(key_of[4], (SEQS, CACHE), 0, 2), jax.random.fold_in(key_of[4], 1), 0, 1).astype(jnp.int32),
        "norm_attn": jnp.clip(0.5 + 1.0 * jax.random.uniform(key_of[5], (2, D), jnp.float32) ** block_scale(key_of[5], (2, D), ((0, 2),), -0.2, 0.2), 0.5, 1.5),
        "query_weight": gaussian(key_of[6], (2, D, D), D ** -0.5, 0.09375, ((0, 2), (1, 4), (2, 4))),
        "query_gain": jnp.clip(jnp.exp(math.log(2.5) - 1.609438 * jax.random.uniform(key_of[7], (2, D), jnp.float32) ** block_scale(key_of[7], (2, D), ((0, 2), (1, 4)), -0.2, 0.2)), 0.5, 2.5),
        "key_gain": jnp.clip(jnp.exp(math.log(2.5) - 1.609438 * jax.random.uniform(key_of[8], (2, D), jnp.float32) ** block_scale(key_of[8], (2, D), ((1, 4),), -0.2, 0.2)), 0.5, 2.5),
        "out_weight": gaussian(key_of[9], (2, D, D), D ** -0.5, 0.09375, ((0, 2), (1, 4), (2, 4))),
        "norm_ffn": jnp.clip(0.5 + 1.0 * jax.random.uniform(key_of[10], (2, D), jnp.float32) ** block_scale(key_of[10], (2, D), ((0, 2),), -0.2, 0.2), 0.5, 1.5),
        "gate_weight": gaussian(key_of[11], (2, D, FF), D ** -0.5, 0.09375, ((0, 2), (1, 4), (2, 4))),
        "up_weight": gaussian(key_of[12], (2, D, FF), D ** -0.5, 0.09375, ((0, 2), (1, 4), (2, 4))),
        "down_weight": gaussian(key_of[13], (2, FF, D), FF ** -0.5, 0.0546875, ((0, 2), (1, 4), (2, 4))),
    }


epsilon = 1e-05

def rms_scale(values, scales):
    inverse = lax.rsqrt(lax.optimization_barrier(jnp.mean(values * values, axis=-1, keepdims=True)) + epsilon)
    return values * inverse * scales

def attend_head(query_head, key_head, value_head, query_pos):
    scores = jnp.dot(query_head, key_head.T, preferred_element_type=jnp.float32) * (1.0 / math.sqrt(HD))
    allowed = jnp.arange(CACHE, dtype=jnp.int32)[None, :] <= query_pos[:, None]
    scores = jnp.where(allowed, scores, -1e+30)
    row_max = lax.optimization_barrier(jnp.max(scores, axis=-1, keepdims=True))
    weights = jnp.exp(scores - row_max)
    row_total = lax.optimization_barrier(jnp.sum(weights, axis=-1, keepdims=True))
    summed = jnp.dot(weights.astype(jnp.bfloat16), value_head, preferred_element_type=jnp.float32)
    return (summed / row_total).astype(jnp.bfloat16)

def reference(hidden_in, query_modality, key_cache, value_cache, key_modality, norm_attn, query_weight, query_gain, key_gain, out_weight, norm_ffn, gate_weight, up_weight, down_weight):
    query_pos = CACHE - SLAB + jnp.arange(SLAB, dtype=jnp.int32)
    outputs = []
    for seq_index in range(SEQS):
        modality_ids = query_modality[seq_index]
        sorted_rows = jnp.argsort(modality_ids, stable=True).astype(jnp.int32)
        group_index = (sorted_rows[:MAIN], sorted_rows[SLAB - MAIN:])
        rows_all = hidden_in[seq_index].astype(jnp.float32)
        queries = jnp.zeros((SLAB, HEADS, HD), jnp.float32)
        for modality in range(2):
            row_index = group_index[modality]
            keep_rows = (modality_ids[row_index] == modality)[:, None, None]
            normed = rms_scale(rows_all[row_index], norm_attn[modality]).astype(jnp.bfloat16)
            projected = jnp.dot(normed, query_weight[modality], preferred_element_type=jnp.float32).reshape(MAIN, HEADS, HD)
            normal_q = rms_scale(projected, query_gain[modality].reshape(HEADS, HD))
            queries = queries.at[row_index].set(jnp.where(keep_rows, normal_q, queries[row_index]))
        queries = queries.astype(jnp.bfloat16)
        key_scale = jnp.where(key_modality[seq_index][:, None] == 0, key_gain[0][None, :], key_gain[1][None, :]).reshape(CACHE, HEADS, HD)
        key_rows = rms_scale(key_cache[seq_index].astype(jnp.float32).reshape(CACHE, HEADS, HD), key_scale).astype(jnp.bfloat16)
        value_rows = value_cache[seq_index].reshape(CACHE, HEADS, HD)
        head_out = lax.map(lambda triple: attend_head(triple[0], triple[1], triple[2], query_pos), (queries.transpose(1, 0, 2), key_rows.transpose(1, 0, 2), value_rows.transpose(1, 0, 2)))
        head_out = head_out.transpose(1, 0, 2).reshape(SLAB, D)
        mixed_rows = jnp.zeros((SLAB, D), jnp.bfloat16)
        for modality in range(2):
            row_index = group_index[modality]
            keep_rows = (modality_ids[row_index] == modality)[:, None]
            attention = jnp.dot(head_out[row_index], out_weight[modality], preferred_element_type=jnp.float32)
            residual = rows_all[row_index] + attention
            normed = rms_scale(residual, norm_ffn[modality]).astype(jnp.bfloat16)
            gate_val = jnp.dot(normed, gate_weight[modality], preferred_element_type=jnp.float32)
            up_val = jnp.dot(normed, up_weight[modality], preferred_element_type=jnp.float32)
            activated = (jax.nn.silu(gate_val) * up_val).astype(jnp.bfloat16)
            result = (residual + jnp.dot(activated, down_weight[modality], preferred_element_type=jnp.float32)).astype(jnp.bfloat16)
            mixed_rows = mixed_rows.at[row_index].set(jnp.where(keep_rows, result, mixed_rows[row_index]))
        outputs.append(mixed_rows)
    return jnp.stack(outputs)
```

```python
import functools
import math

import jax
import jax.numpy as jnp
from jax import lax
from jax.experimental import pallas as pl
from jax.experimental.pallas import tpu as pltpu
from jax.sharding import PartitionSpec as P

HD = 128
LANES = 128

epsilon = 1e-05
bf16 = jnp.bfloat16
f32 = jnp.float32


def exchange_kernel(axis, n, gather, x_ref, o_ref, send_sems, recv_sems, own_sem):
    me = lax.axis_index(axis)
    barrier = pltpu.get_barrier_semaphore()
    for step in range(1, n):
        pl.semaphore_signal(
            barrier,
            inc=1,
            device_id={axis: lax.rem(me + step, n)},
            device_id_type=pl.DeviceIdType.MESH,
        )
    pl.semaphore_wait(barrier, n - 1)
    copies = []
    for step in range(1, n):
        peer = lax.rem(me + step, n)
        copy = pltpu.make_async_remote_copy(
            src_ref=x_ref if gather else x_ref.at[peer],
            dst_ref=o_ref.at[me],
            send_sem=send_sems.at[step],
            recv_sem=recv_sems.at[step],
            device_id={axis: peer},
            device_id_type=pl.DeviceIdType.MESH,
        )
        copy.start()
        copies.append(copy)
    own = pltpu.make_async_copy(x_ref if gather else x_ref.at[me], o_ref.at[me], own_sem)
    own.start()
    own.wait()
    for copy in copies:
        copy.wait()


def exchange(x, axis, call_id, gather=False):
    n = lax.axis_size(axis)
    shape = (n,) + x.shape if gather else x.shape
    return pl.pallas_call(
        functools.partial(exchange_kernel, axis, n, gather),
        out_shape=jax.ShapeDtypeStruct(shape, x.dtype),
        in_specs=[pl.BlockSpec(memory_space=pltpu.VMEM)],
        out_specs=pl.BlockSpec(memory_space=pltpu.VMEM),
        scratch_shapes=[
            pltpu.SemaphoreType.DMA((n,)),
            pltpu.SemaphoreType.DMA((n,)),
            pltpu.SemaphoreType.DMA,
        ],
        compiler_params=pltpu.CompilerParams(collective_id=call_id, has_side_effects=True),
        name=f"exchange_{call_id}_{axis}",
    )(x)


def attend_kernel(heads, rows, chunk, first_free, at_ref, q_ref, k_ref, v_ref, m_ref, o_ref, acc, total):
    step = pl.program_id(0)

    @pl.when(step == 0)
    def _():
        acc[...] = jnp.zeros_like(acc)
        total[...] = jnp.zeros_like(total)

    is_first = m_ref[...] == 0
    key_pos = step * chunk + lax.broadcasted_iota(jnp.int32, (rows, chunk), 1)
    row_pos = first_free + at_ref[1] + lax.broadcasted_iota(jnp.int32, (rows, chunk), 0)
    allowed = key_pos <= row_pos
    ones = jnp.ones((8, HD), bf16)
    over_width = (((1,), (1,)), ((), ()))
    for head in range(heads):
        cut = slice(head * HD, (head + 1) * HD)
        keys = k_ref[:, cut]
        both = lax.dot_general(q_ref[head], keys, over_width, preferred_element_type=f32)
        wide = keys.astype(f32)
        squares = lax.dot_general(
            ones, (wide * wide).astype(bf16), over_width, preferred_element_type=f32
        )[:1]
        inverse = lax.rsqrt(squares * (1.0 / HD) + epsilon)
        scores = jnp.where(is_first, both[:rows], both[rows:]) * inverse
        probs = jnp.where(allowed, jnp.exp(scores), 0.0)
        total[head] += jnp.sum(probs, axis=1, keepdims=True)
        acc[head] += jnp.dot(probs.astype(bf16), v_ref[:, cut], preferred_element_type=f32)

    @pl.when(step == pl.num_programs(0) - 1)
    def _():
        for head in range(heads):
            o_ref[:, head * HD : (head + 1) * HD] = (acc[head] / total[head]).astype(bf16)


def attend(queries, key_cache, value_cache, key_modality, column, row_start, slab_len):
    heads, double, _ = queries.shape
    rows = double // 2
    cache_len = key_cache.shape[0]
    chunk = min(1024, cache_len)
    width = heads * HD
    where_at = jnp.stack([column, row_start]).astype(jnp.int32)
    return pl.pallas_call(
        functools.partial(attend_kernel, heads, rows, chunk, cache_len - slab_len),
        out_shape=jax.ShapeDtypeStruct((rows, width), bf16),
        grid_spec=pltpu.PrefetchScalarGridSpec(
            num_scalar_prefetch=1,
            grid=(cache_len // chunk,),
            in_specs=[
                pl.BlockSpec((heads, double, HD), lambda j, at: (0, 0, 0)),
                pl.BlockSpec((chunk, width), lambda j, at: (j, at[0])),
                pl.BlockSpec((chunk, width), lambda j, at: (j, at[0])),
                pl.BlockSpec((1, chunk), lambda j, at: (0, j)),
            ],
            out_specs=pl.BlockSpec((rows, width), lambda j, at: (0, 0)),
            scratch_shapes=[
                pltpu.VMEM((heads, rows, HD), f32),
                pltpu.VMEM((heads, rows, 1), f32),
            ],
        ),
        compiler_params=pltpu.CompilerParams(dimension_semantics=("arbitrary",)),
        name="attend",
    )(where_at, queries, key_cache, value_cache, key_modality)


def two_parts(values):
    high = values.astype(bf16)
    return high, (values - high.astype(f32)).astype(bf16)


def beside(values, columns):
    extra = jnp.stack([c.astype(bf16) for c in columns], axis=-1)
    pad = [(0, 0)] * (extra.ndim - 1) + [(0, LANES - extra.shape[-1])]
    return jnp.concatenate([values.astype(bf16), jnp.pad(extra, pad)], axis=-1)


def per_device(
    hidden_in,
    query_modality,
    key_cache,
    value_cache,
    key_modality,
    norm_attn,
    query_weight,
    query_gain,
    key_gain,
    out_weight,
    norm_ffn,
    gate_weight,
    up_weight,
    down_weight,
):
    m = lax.axis_index("mod")
    d = lax.axis_index("dp")
    n_mod, n_ctx, n_dp = lax.axis_size("mod"), lax.axis_size("ctx"), lax.axis_size("dp")
    rows, model = hidden_in.shape[1:]
    part = model // n_dp
    width = query_weight.shape[2]
    hidden_units = gate_weight.shape[2]
    heads = width // HD
    slab_len = n_mod * n_ctx * rows
    by_heads = heads % n_mod == 0

    hidden = hidden_in[0]
    wide = hidden.astype(f32)
    inverse = lax.rsqrt(jnp.mean(wide * wide, axis=-1) + epsilon)
    sent = jnp.broadcast_to(
        beside(jnp.zeros((rows, 0), bf16), (query_modality[0], *two_parts(inverse)))[None],
        (n_dp, rows, LANES),
    )
    pieces = hidden.reshape(rows, n_dp, part).transpose(1, 0, 2)
    own_block = exchange(jnp.concatenate([pieces, sent], axis=-1), "dp", 0)
    slab = exchange(own_block, "ctx", 1, gather=True)
    slab = exchange(slab, "mod", 2, gather=True)
    tags = slab[..., part : part + 3].astype(f32)
    ids = tags[..., 0]
    is_mine = ids == m.astype(f32)

    gain = lax.dynamic_slice_in_dim(norm_attn[0], d * part, part)
    row_inverse = (tags[..., 1] + tags[..., 2])[..., None]
    normed = jnp.where(
        is_mine[..., None], slab[..., :part].astype(f32) * row_inverse * gain, 0.0
    ).astype(bf16)
    tokens = n_dp * slab_len
    projected = jnp.dot(
        normed.reshape(tokens, part), query_weight[0], preferred_element_type=f32
    ).astype(bf16)
    gains = jnp.pad(jnp.stack(two_parts(query_gain[0])), ((0, 14), (0, 0)))
    if by_heads:
        to_mod = (
            jnp.concatenate([projected, gains], axis=0)
            .reshape(tokens + 16, n_mod, width // n_mod)
            .transpose(1, 0, 2)
        )
    else:
        to_mod = jnp.concatenate(
            [
                projected.reshape(n_mod, tokens // n_mod, width),
                jnp.broadcast_to(gains[None], (n_mod, 16, width)),
            ],
            axis=1,
        )
    from_mod = exchange(to_mod, "mod", 3).astype(f32)
    split_width = from_mod.shape[-1]
    both_gains = from_mod[:, -16] + from_mod[:, -15]
    blocks = n_ctx * n_mod if by_heads else n_ctx
    to_dp = (
        jnp.sum(from_mod[:, :-16], axis=0)
        .astype(bf16)
        .reshape(blocks, n_dp, rows, split_width)
        .transpose(1, 0, 2, 3)
        .reshape(n_dp, blocks * rows, split_width)
    )
    projected = jnp.sum(exchange(to_dp, "dp", 4).astype(f32), axis=0)
    count = blocks * rows
    split_heads = split_width // HD
    own_ids = lax.dynamic_index_in_dim(ids, d, 2, keepdims=False)
    if by_heads:
        own_ids = own_ids.reshape(count)
        column, row_start = m, jnp.int32(0)
        key_gains = lax.dynamic_slice_in_dim(key_gain, m * split_width, split_width, 1)
    else:
        own_ids = lax.dynamic_index_in_dim(own_ids, m, 0, keepdims=False).reshape(count)
        column, row_start = jnp.int32(0), m * count
        key_gains = key_gain
    token_gain = jnp.where(own_ids[:, None] == 0, both_gains[0][None], both_gains[1][None])
    by_head = projected.reshape(count, split_heads, HD)
    by_head = by_head * lax.rsqrt(
        jnp.mean(by_head * by_head, axis=-1, keepdims=True) + epsilon
    )
    by_head = by_head * token_gain.reshape(count, split_heads, HD) * (1.0 / math.sqrt(HD))
    queries = by_head[None] * key_gains.reshape(2, 1, split_heads, HD)
    queries = (
        queries.astype(bf16).transpose(2, 0, 1, 3).reshape(split_heads, 2 * count, HD)
    )
    head_out = attend(
        queries, key_cache[0], value_cache[0], key_modality, column, row_start, slab_len
    )

    shared = exchange(head_out, "dp", 5, gather=True)
    shared = exchange(shared, "mod", 6, gather=True)
    if by_heads:
        shared = shared.transpose(1, 2, 0, 3).reshape(n_dp, n_mod, n_ctx * rows, width)
        shared = shared.transpose(1, 0, 2, 3)
    ids_mdcr = is_mine.transpose(0, 2, 1, 3).reshape(n_mod, n_dp, n_ctx * rows, 1)

    def to_blocks(values, weight, first_id):
        masked = jnp.where(ids_mdcr, values, jnp.zeros_like(values))
        product = jnp.dot(
            masked.reshape(tokens, values.shape[-1]), weight, preferred_element_type=f32
        ).astype(bf16)
        product = product.reshape(n_mod, n_dp * n_ctx * rows, part)
        product = exchange(product, "mod", first_id).astype(f32)
        product = (
            jnp.sum(product, axis=0)
            .astype(bf16)
            .reshape(n_dp, n_ctx, rows, part)
            .transpose(1, 0, 2, 3)
        )
        return jnp.sum(exchange(product, "ctx", first_id + 1).astype(f32), axis=0)

    attention = to_blocks(shared, out_weight[0], 7)
    residual = own_block[..., :part].astype(f32) + attention
    squares = jnp.sum(residual * residual, axis=-1)

    slab = exchange(beside(residual, two_parts(squares)), "ctx", 9, gather=True)
    slab = exchange(slab, "mod", 10, gather=True)
    gain = lax.dynamic_slice_in_dim(norm_ffn[0], d * part, part)
    scaled = jnp.where(is_mine[..., None], slab[..., :part].astype(f32) * gain, 0.0)
    scaled = scaled.astype(bf16).reshape(tokens, part)
    gate = jnp.dot(scaled, gate_weight[0], preferred_element_type=f32).astype(bf16)
    up = jnp.dot(scaled, up_weight[0], preferred_element_type=f32).astype(bf16)

    def over_mod(values, call_id):
        values = values.reshape(n_mod, tokens // n_mod, hidden_units)
        values = jnp.sum(exchange(values, "mod", call_id).astype(f32), axis=0).astype(bf16)
        values = values.reshape(n_ctx, n_dp, rows, hidden_units).transpose(1, 0, 2, 3)
        return values.reshape(n_dp, n_ctx * rows, hidden_units)

    own_squares = lax.dynamic_index_in_dim(slab[..., part : part + 2], m, 0, keepdims=False)
    own_squares = own_squares.transpose(1, 0, 2, 3).reshape(n_dp, n_ctx * rows, 2)
    own_squares = jnp.pad(own_squares, ((0, 0), (0, 0), (0, LANES - 2)))
    to_dp = jnp.concatenate([over_mod(gate, 11), own_squares], axis=-1)
    gate = jnp.sum(exchange(to_dp, "dp", 12).astype(f32), axis=0)
    up = jnp.sum(exchange(over_mod(up, 13), "dp", 14).astype(f32), axis=0)
    squares = gate[:, hidden_units : hidden_units + 1] + gate[:, hidden_units + 1 : hidden_units + 2]
    inverse = lax.rsqrt(squares * (1.0 / model) + epsilon)
    activated = (jax.nn.silu(gate[:, :hidden_units] * inverse) * (up * inverse)).astype(bf16)
    shared = exchange(activated, "dp", 15, gather=True)
    shared = exchange(shared, "mod", 16, gather=True)
    mixed = residual + to_blocks(shared, down_weight[0], 17)
    home = exchange(mixed.astype(bf16), "dp", 19)
    return home.transpose(1, 0, 2).reshape(1, rows, model)


def solution(mesh):
    placed = (
        P("dp", ("mod", "ctx"), None),
        P("dp", ("mod", "ctx")),
        P("dp", None, "ctx"),
        P("dp", None, "ctx"),
        P("dp", None),
        P("mod", None),
        P("mod", "dp", "ctx"),
        P("mod", "ctx"),
        P(None, "ctx"),
        P("mod", "ctx", "dp"),
        P("mod", None),
        P("mod", "dp", "ctx"),
        P("mod", "dp", "ctx"),
        P("mod", "ctx", "dp"),
    )
    return jax.shard_map(
        per_device,
        mesh=mesh,
        in_specs=placed,
        out_specs=P("dp", ("mod", "ctx"), None),
        check_vma=False,
    )
```

```python
import functools
import math

import jax
import jax.numpy as jnp
from jax import lax
from jax.experimental import pallas as pl
from jax.experimental.pallas import tpu as pltpu
from jax.sharding import PartitionSpec as P

HD = 128
LANES = 128

epsilon = 1e-05
bf16 = jnp.bfloat16
f32 = jnp.float32


def greet(axes):
    barrier = pltpu.get_barrier_semaphore()
    count = 0
    for axis in axes:
        me, n = lax.axis_index(axis), lax.axis_size(axis)
        for step in range(1, n):
            pl.semaphore_signal(
                barrier,
                inc=1,
                device_id={axis: lax.rem(me + step, n)},
                device_id_type=pl.DeviceIdType.MESH,
            )
        count += n - 1
    pl.semaphore_wait(barrier, count)


def send(source, target, sems, slot, axis, peer):
    copy = pltpu.make_async_remote_copy(
        src_ref=source,
        dst_ref=target,
        send_sem=sems[0].at[slot],
        recv_sem=sems[1].at[slot],
        device_id={axis: peer},
        device_id_type=pl.DeviceIdType.MESH,
    )
    copy.start()
    return copy


def copy_here(source, target, sem):
    copy = pltpu.make_async_copy(source, target, sem)
    copy.start()
    copy.wait()


def swap_all(axis, source_of, target_of, sems, own_sem):
    me, n = lax.axis_index(axis), lax.axis_size(axis)
    copies = []
    for step in range(1, n):
        peer = lax.rem(me + step, n)
        copies.append(send(source_of(peer), target_of(me), sems, step, axis, peer))
    copy_here(source_of(me), target_of(me), own_sem)
    for copy in copies:
        copy.wait()


def spread(axis, source, place, sems, relay_sems, own_sem):
    me, n = lax.axis_index(axis), lax.axis_size(axis)
    m, n_mod = lax.axis_index("mod"), lax.axis_size("mod")
    copies, relays = [], []
    for step in range(1, n):
        peer = lax.rem(me + step, n)
        copies.append(send(source, place(m, me), sems, step, axis, peer))

    def relay(block, origin, step):
        for other in range(1, n_mod):
            partner = lax.rem(m + other, n_mod)
            slot = (other - 1) * n + step
            relays.append(send(block, place(m, origin), relay_sems, slot, "mod", partner))

    relay(source, me, 0)
    copy_here(source, place(m, me), own_sem)
    for step in range(1, n):
        copies[step - 1].wait_recv()
        origin = lax.rem(me + n - step, n)
        relay(place(m, origin), origin, step)
    for copy in copies:
        copy.wait_send()
    for copy in relays:
        copy.wait()


def dma_sems(*counts):
    return [pltpu.SemaphoreType.DMA((count,)) for count in counts for _ in range(2)]


def communicate(kernel, call_id, name, operands, outs, scratch):
    whole = pl.BlockSpec(memory_space=pltpu.VMEM)
    return pl.pallas_call(
        kernel,
        out_shape=outs,
        in_specs=[whole] * len(operands),
        out_specs=[whole] * len(outs),
        scratch_shapes=scratch,
        compiler_params=pltpu.CompilerParams(
            collective_id=call_id, has_side_effects=True, vmem_limit_bytes=60 * 2**20
        ),
        name=name,
    )(*operands)


def enter_kernel(x_ref, block_ref, o_ref, s0, r0, s1, r1, s2, r2, own_sem):
    greet(("dp", "ctx", "mod"))
    swap_all("dp", lambda i: x_ref.at[i], lambda i: block_ref.at[i], (s0, r0), own_sem)
    spread("ctx", block_ref, lambda j, i: o_ref.at[:, j, i], (s1, r1), (s2, r2), own_sem)


def enter(x, call_id):
    n_dp, rows, cols = x.shape
    n_mod, n_ctx = lax.axis_size("mod"), lax.axis_size("ctx")
    return communicate(
        enter_kernel,
        call_id,
        "enter",
        (x,),
        [
            jax.ShapeDtypeStruct(x.shape, x.dtype),
            jax.ShapeDtypeStruct((n_dp, n_mod, n_ctx, rows, cols), x.dtype),
        ],
        dma_sems(n_dp, n_ctx, n_mod * n_ctx) + [pltpu.SemaphoreType.DMA],
    )


def gather(x, axis, shape, place, call_id):
    n_mod, n = lax.axis_size("mod"), lax.axis_size(axis)

    def kernel(x_ref, o_ref, s1, r1, s2, r2, own_sem):
        greet((axis, "mod"))
        spread(axis, x_ref, lambda j, i: place(o_ref, j, i), (s1, r1), (s2, r2), own_sem)

    return communicate(
        kernel,
        call_id,
        f"gather_{call_id}_{axis}",
        (x,),
        [jax.ShapeDtypeStruct(shape, x.dtype)],
        dma_sems(n, n_mod * n) + [pltpu.SemaphoreType.DMA],
    )[0]


def home_kernel(x_ref, o_ref, s0, r0, own_sem):
    greet(("dp",))
    swap_all("dp", lambda i: x_ref.at[i], lambda i: o_ref.at[i], (s0, r0), own_sem)


def to_home(x, call_id):
    return communicate(
        home_kernel,
        call_id,
        "to_home",
        (x,),
        [jax.ShapeDtypeStruct(x.shape, x.dtype)],
        dma_sems(x.shape[0]) + [pltpu.SemaphoreType.DMA],
    )[0]


def reduce_kernel(axis, count, block, *refs):
    me, n = lax.axis_index(axis), lax.axis_size(axis)
    m, n_mod = lax.axis_index("mod"), lax.axis_size("mod")
    xs, outs = refs[:count], refs[count : 2 * count]
    near, far, land = (refs[(2 + i) * count : (3 + i) * count] for i in range(3))
    s1, r1, s2, r2 = refs[5 * count :]
    greet((axis, "mod"))
    order = list(range(1, n)) + [0]
    swaps, copies = {}, []
    for step in order:
        peer = lax.rem(me + step, n)
        for which in range(count):
            for other in range(1, n_mod):
                partner = lax.rem(m + other, n_mod)
                slot = ((other - 1) * n + step) * count + which
                swaps[step, which, other] = send(
                    block(xs[which], partner, peer),
                    near[which].at[other - 1, step],
                    (s1, r1),
                    slot,
                    "mod",
                    partner,
                )

    def over_mod(step, which):
        total = block(xs[which], m, lax.rem(me + step, n))[...].astype(f32)
        for other in range(1, n_mod):
            swaps[step, which, other].wait_recv()
            total += near[which][other - 1, step].astype(f32)
        return total

    for step in range(1, n):
        for which in range(count):
            far[which][step] = over_mod(step, which).astype(bf16)
            copies.append(
                send(
                    far[which].at[step],
                    land[which].at[step],
                    (s2, r2),
                    step * count + which,
                    axis,
                    lax.rem(me + step, n),
                )
            )
    for which in range(count):
        outs[which][...] = over_mod(0, which)
    for index, copy in enumerate(copies):
        copy.wait_recv()
        step, which = 1 + index // count, index % count
        outs[which][...] += land[which][step].astype(f32)
    for copy in copies:
        copy.wait_send()
    for copy in swaps.values():
        copy.wait_send()


def reduce(xs, axis, block, block_shapes, call_id):
    n_mod, n, count = lax.axis_size("mod"), lax.axis_size(axis), len(xs)
    slots = [pltpu.VMEM((n_mod - 1, n) + shape, bf16) for shape in block_shapes]
    lines = [pltpu.VMEM((n,) + shape, bf16) for shape in block_shapes]
    return communicate(
        functools.partial(reduce_kernel, axis, count, block),
        call_id,
        f"reduce_{call_id}_{axis}",
        xs,
        [jax.ShapeDtypeStruct(shape, f32) for shape in block_shapes],
        slots + lines + lines + dma_sems(n_mod * n * count, n * count),
    )


def attend_kernel(heads, rows, chunk, first_free, at_ref, q_ref, k_ref, v_ref, m_ref, o_ref, acc, total):
    step = pl.program_id(0)

    @pl.when(step == 0)
    def _():
        acc[...] = jnp.zeros_like(acc)
        total[...] = jnp.zeros_like(total)

    ones = jnp.ones((8, HD), bf16)
    over_width = (((1,), (1,)), ((), ()))

    def add_chunk(masked):
        is_first = m_ref[...] == 0
        for head in range(heads):
            cut = slice(head * HD, (head + 1) * HD)
            keys = k_ref[:, cut]
            both = lax.dot_general(q_ref[head], keys, over_width, preferred_element_type=f32)
            wide = keys.astype(f32)
            squares = lax.dot_general(
                ones, (wide * wide).astype(bf16), over_width, preferred_element_type=f32
            )[:1]
            inverse = lax.rsqrt(squares * (1.0 / HD) + epsilon)
            probs = jnp.exp(jnp.where(is_first, both[:rows], both[rows:]) * inverse)
            if masked:
                key_pos = step * chunk + lax.broadcasted_iota(jnp.int32, (rows, chunk), 1)
                row_pos = lax.broadcasted_iota(jnp.int32, (rows, chunk), 0)
                probs = jnp.where(key_pos <= first_free + at_ref[1] + row_pos, probs, 0.0)
            total[head] += jnp.sum(probs, axis=1, keepdims=True)
            acc[head] += jnp.dot(probs.astype(bf16), v_ref[:, cut], preferred_element_type=f32)

    has_free = (step + 1) * chunk > first_free

    @pl.when(has_free)
    def _():
        add_chunk(True)

    @pl.when(jnp.logical_not(has_free))
    def _():
        add_chunk(False)

    @pl.when(step == pl.num_programs(0) - 1)
    def _():
        for head in range(heads):
            o_ref[:, head * HD : (head + 1) * HD] = (acc[head] / total[head]).astype(bf16)


def attend(queries, key_cache, value_cache, key_modality, column, row_start, slab_len):
    heads, double, _ = queries.shape
    rows = double // 2
    cache_len = key_cache.shape[0]
    chunk = min(1024, cache_len)
    width = heads * HD
    where_at = jnp.stack([column, row_start]).astype(jnp.int32)
    return pl.pallas_call(
        functools.partial(attend_kernel, heads, rows, chunk, cache_len - slab_len),
        out_shape=jax.ShapeDtypeStruct((rows, width), bf16),
        grid_spec=pltpu.PrefetchScalarGridSpec(
            num_scalar_prefetch=1,
            grid=(cache_len // chunk,),
            in_specs=[
                pl.BlockSpec((heads, double, HD), lambda j, at: (0, 0, 0)),
                pl.BlockSpec((chunk, width), lambda j, at: (j, at[0])),
                pl.BlockSpec((chunk, width), lambda j, at: (j, at[0])),
                pl.BlockSpec((1, chunk), lambda j, at: (0, j)),
            ],
            out_specs=pl.BlockSpec((rows, width), lambda j, at: (0, 0)),
            scratch_shapes=[
                pltpu.VMEM((heads, rows, HD), f32),
                pltpu.VMEM((heads, rows, 1), f32),
            ],
        ),
        compiler_params=pltpu.CompilerParams(dimension_semantics=("arbitrary",)),
        name="attend",
    )(where_at, queries, key_cache, value_cache, key_modality)


def two_parts(values):
    high = values.astype(bf16)
    return high, (values - high.astype(f32)).astype(bf16)


def beside(values, columns):
    extra = jnp.stack([c.astype(bf16) for c in columns], axis=-1)
    pad = [(0, 0)] * (extra.ndim - 1) + [(0, LANES - extra.shape[-1])]
    return jnp.concatenate([values.astype(bf16), jnp.pad(extra, pad)], axis=-1)


def per_device(
    hidden_in,
    query_modality,
    key_cache,
    value_cache,
    key_modality,
    norm_attn,
    query_weight,
    query_gain,
    key_gain,
    out_weight,
    norm_ffn,
    gate_weight,
    up_weight,
    down_weight,
):
    m = lax.axis_index("mod")
    d = lax.axis_index("dp")
    n_mod, n_ctx, n_dp = lax.axis_size("mod"), lax.axis_size("ctx"), lax.axis_size("dp")
    rows, model = hidden_in.shape[1:]
    part = model // n_dp
    width = query_weight.shape[2]
    hidden_units = gate_weight.shape[2]
    heads = width // HD
    slab_len = n_mod * n_ctx * rows
    by_heads = heads % n_mod == 0

    hidden = hidden_in[0]
    wide = hidden.astype(f32)
    inverse = lax.rsqrt(jnp.mean(wide * wide, axis=-1) + epsilon)
    sent = jnp.broadcast_to(
        beside(jnp.zeros((rows, 0), bf16), (query_modality[0], *two_parts(inverse)))[None],
        (n_dp, rows, LANES),
    )
    pieces = hidden.reshape(rows, n_dp, part).transpose(1, 0, 2)
    own_block, slab = enter(jnp.concatenate([pieces, sent], axis=-1), 0)
    tags = slab[..., part : part + 3].astype(f32)
    ids = tags[..., 0]
    is_mine = ids == m.astype(f32)

    gain = lax.dynamic_slice_in_dim(norm_attn[0], d * part, part)
    row_inverse = (tags[..., 1] + tags[..., 2])[..., None]
    normed = jnp.where(
        is_mine[..., None], slab[..., :part].astype(f32) * row_inverse * gain, 0.0
    ).astype(bf16)
    tokens = n_dp * slab_len
    projected = jnp.dot(
        normed.reshape(tokens, part), query_weight[0], preferred_element_type=f32
    ).astype(bf16)
    gains = jnp.stack(two_parts(query_gain[0]))
    gains = jnp.where(jnp.arange(n_mod)[:, None, None] == m, gains[None], jnp.zeros_like(gains)[None])
    gains = jnp.pad(gains.reshape(2 * n_mod, width), ((0, 16 - 2 * n_mod), (0, 0)))
    gains = jnp.where(d == 0, gains, jnp.zeros_like(gains))
    split_width = width // n_mod if by_heads else width
    blocks = n_ctx * n_mod if by_heads else n_ctx
    count = blocks * rows
    if by_heads:
        to_sum = jnp.concatenate(
            [
                projected.reshape(n_dp, count, width),
                jnp.broadcast_to(gains[None], (n_dp, 16, width)),
            ],
            axis=1,
        )
        to_sum = to_sum.reshape(n_dp, count + 16, n_mod, split_width).transpose(0, 2, 1, 3)
    else:
        to_sum = jnp.concatenate(
            [
                projected.reshape(n_dp, n_mod, count, width),
                jnp.broadcast_to(gains[None, None], (n_dp, n_mod, 16, width)),
            ],
            axis=2,
        )
    (summed,) = reduce(
        (to_sum,), "dp", lambda ref, j, i: ref.at[i, j], [(count + 16, split_width)], 1
    )
    projected = summed[:count]
    both_gains = summed[count : count + 2 * n_mod : 2] + summed[count + 1 : count + 2 * n_mod : 2]
    split_heads = split_width // HD
    own_ids = lax.dynamic_index_in_dim(ids, d, 0, keepdims=False)
    if by_heads:
        own_ids = own_ids.reshape(count)
        column, row_start = m, jnp.int32(0)
        key_gains = lax.dynamic_slice_in_dim(key_gain, m * split_width, split_width, 1)
    else:
        own_ids = lax.dynamic_index_in_dim(own_ids, m, 0, keepdims=False).reshape(count)
        column, row_start = jnp.int32(0), m * count
        key_gains = key_gain
    token_gain = jnp.where(own_ids[:, None] == 0, both_gains[0][None], both_gains[1][None])
    by_head = projected.reshape(count, split_heads, HD)
    by_head = by_head * lax.rsqrt(
        jnp.mean(by_head * by_head, axis=-1, keepdims=True) + epsilon
    )
    by_head = by_head * token_gain.reshape(count, split_heads, HD) * (1.0 / math.sqrt(HD))
    queries = by_head[None] * key_gains.reshape(2, 1, split_heads, HD)
    queries = (
        queries.astype(bf16).transpose(2, 0, 1, 3).reshape(split_heads, 2 * count, HD)
    )
    head_out = attend(
        queries, key_cache[0], value_cache[0], key_modality, column, row_start, slab_len
    )

    if by_heads:
        shared = gather(
            head_out,
            "dp",
            (n_dp, count, width),
            lambda ref, j, i: ref.at[i, :, pl.ds(pl.multiple_of(j * split_width, LANES), split_width)],
            2,
        )
    else:
        shared = gather(
            head_out, "dp", (n_dp, n_mod, count, width), lambda ref, j, i: ref.at[i, j], 2
        )

    def to_blocks(values, weight, call_id):
        values = values.reshape(tokens, values.shape[-1])
        masked = jnp.where(is_mine.reshape(tokens, 1), values, jnp.zeros_like(values))
        product = jnp.dot(masked, weight, preferred_element_type=f32).astype(bf16)
        product = product.reshape(n_dp, n_mod, n_ctx, rows, part)
        return reduce(
            (product,), "ctx", lambda ref, j, i: ref.at[:, j, i], [(n_dp, rows, part)], call_id
        )[0]

    attention = to_blocks(shared, out_weight[0], 3)
    residual = own_block[..., :part].astype(f32) + attention
    squares = jnp.sum(residual * residual, axis=-1)

    slab = gather(
        beside(residual, two_parts(squares)),
        "ctx",
        (n_dp, n_mod, n_ctx, rows, part + LANES),
        lambda ref, j, i: ref.at[:, j, i],
        4,
    )
    gain = lax.dynamic_slice_in_dim(norm_ffn[0], d * part, part)
    scaled = jnp.where(is_mine[..., None], slab[..., :part].astype(f32) * gain, 0.0)
    scaled = scaled.astype(bf16).reshape(tokens, part)
    by_block = (n_dp, n_mod, n_ctx * rows)
    gate = jnp.dot(scaled, gate_weight[0], preferred_element_type=f32).astype(bf16)
    up = jnp.dot(scaled, up_weight[0], preferred_element_type=f32).astype(bf16)
    squares = jnp.where(is_mine[..., None], slab[..., part:], jnp.zeros_like(slab[..., part:]))
    gate, up, squares = reduce(
        (
            gate.reshape(*by_block, hidden_units),
            up.reshape(*by_block, hidden_units),
            squares.reshape(*by_block, LANES),
        ),
        "dp",
        lambda ref, j, i: ref.at[i, j],
        [(n_ctx * rows, hidden_units)] * 2 + [(n_ctx * rows, LANES)],
        5,
    )
    inverse = lax.rsqrt((squares[:, :1] + squares[:, 1:2]) * (1.0 / model) + epsilon)
    activated = (jax.nn.silu(gate * inverse) * (up * inverse)).astype(bf16)
    shared = gather(
        activated, "dp", (*by_block, hidden_units), lambda ref, j, i: ref.at[i, j], 6
    )
    mixed = residual + to_blocks(shared, down_weight[0], 7)
    home = to_home(mixed.astype(bf16), 8)
    return home.transpose(1, 0, 2).reshape(1, rows, model)


def solution(mesh):
    placed = (
        P("dp", ("mod", "ctx"), None),
        P("dp", ("mod", "ctx")),
        P("dp", None, "ctx"),
        P("dp", None, "ctx"),
        P("dp", None),
        P("mod", None),
        P("mod", "dp", "ctx"),
        P("mod", "ctx"),
        P(None, "ctx"),
        P("mod", "ctx", "dp"),
        P("mod", None),
        P("mod", "dp", "ctx"),
        P("mod", "dp", "ctx"),
        P("mod", "ctx", "dp"),
    )
    return jax.shard_map(
        per_device,
        mesh=mesh,
        in_specs=placed,
        out_specs=P("dp", ("mod", "ctx"), None),
        check_vma=False,
    )
```

```python
import functools
import math

import jax
import jax.numpy as jnp
from jax import lax
from jax.experimental import pallas as pl
from jax.experimental.pallas import tpu as pltpu
from jax.sharding import PartitionSpec as P

HD = 128
LANES = 128

epsilon = 1e-05
bf16 = jnp.bfloat16
f32 = jnp.float32


def greet(axes):
    barrier = pltpu.get_barrier_semaphore()
    count = 0
    for axis in axes:
        me, n = lax.axis_index(axis), lax.axis_size(axis)
        for step in range(1, n):
            pl.semaphore_signal(
                barrier,
                inc=1,
                device_id={axis: lax.rem(me + step, n)},
                device_id_type=pl.DeviceIdType.MESH,
            )
        count += n - 1
    pl.semaphore_wait(barrier, count)


def send(source, target, sems, slot, axis, peer):
    copy = pltpu.make_async_remote_copy(
        src_ref=source,
        dst_ref=target,
        send_sem=sems[0].at[slot],
        recv_sem=sems[1].at[slot],
        device_id={axis: peer},
        device_id_type=pl.DeviceIdType.MESH,
    )
    copy.start()
    return copy


def copy_here(source, target, sem):
    copy = pltpu.make_async_copy(source, target, sem)
    copy.start()
    copy.wait()


def swap_all(axis, source_of, target_of, sems, own_sem):
    me, n = lax.axis_index(axis), lax.axis_size(axis)
    copies = []
    for step in range(1, n):
        peer = lax.rem(me + step, n)
        copies.append(send(source_of(peer), target_of(me), sems, step, axis, peer))
    copy_here(source_of(me), target_of(me), own_sem)
    for copy in copies:
        copy.wait()


def spread(axis, source, place, sems, relay_sems, own_sem):
    me, n = lax.axis_index(axis), lax.axis_size(axis)
    m, n_mod = lax.axis_index("mod"), lax.axis_size("mod")
    copies, relays = [], []
    for step in range(1, n):
        peer = lax.rem(me + step, n)
        copies.append(send(source, place(m, me), sems, step, axis, peer))

    def relay(block, origin, step):
        for other in range(1, n_mod):
            partner = lax.rem(m + other, n_mod)
            slot = (other - 1) * n + step
            relays.append(send(block, place(m, origin), relay_sems, slot, "mod", partner))

    relay(source, me, 0)
    copy_here(source, place(m, me), own_sem)
    for step in range(1, n):
        copies[step - 1].wait_recv()
        origin = lax.rem(me + n - step, n)
        relay(place(m, origin), origin, step)
    for copy in copies:
        copy.wait_send()
    for copy in relays:
        copy.wait()


def dma_sems(*counts):
    return [pltpu.SemaphoreType.DMA((count,)) for count in counts for _ in range(2)]


def communicate(kernel, call_id, name, operands, outs, scratch):
    whole = pl.BlockSpec(memory_space=pltpu.VMEM)
    return pl.pallas_call(
        kernel,
        out_shape=outs,
        in_specs=[whole] * len(operands),
        out_specs=[whole] * len(outs),
        scratch_shapes=scratch,
        compiler_params=pltpu.CompilerParams(
            collective_id=call_id, has_side_effects=True, vmem_limit_bytes=60 * 2**20
        ),
        name=name,
    )(*operands)


def enter_kernel(x_ref, block_ref, o_ref, s0, r0, s1, r1, s2, r2, own_sem):
    greet(("dp", "ctx", "mod"))
    swap_all("dp", lambda i: x_ref.at[i], lambda i: block_ref.at[i], (s0, r0), own_sem)
    spread("ctx", block_ref, lambda j, i: o_ref.at[:, j, i], (s1, r1), (s2, r2), own_sem)


def enter(x, call_id):
    n_dp, rows, cols = x.shape
    n_mod, n_ctx = lax.axis_size("mod"), lax.axis_size("ctx")
    return communicate(
        enter_kernel,
        call_id,
        "enter",
        (x,),
        [
            jax.ShapeDtypeStruct(x.shape, x.dtype),
            jax.ShapeDtypeStruct((n_dp, n_mod, n_ctx, rows, cols), x.dtype),
        ],
        dma_sems(n_dp, n_ctx, n_mod * n_ctx) + [pltpu.SemaphoreType.DMA],
    )


def gather(x, axis, shape, place, call_id):
    n_mod, n = lax.axis_size("mod"), lax.axis_size(axis)

    def kernel(x_ref, o_ref, s1, r1, s2, r2, own_sem):
        greet((axis, "mod"))
        spread(axis, x_ref, lambda j, i: place(o_ref, j, i), (s1, r1), (s2, r2), own_sem)

    return communicate(
        kernel,
        call_id,
        f"gather_{call_id}_{axis}",
        (x,),
        [jax.ShapeDtypeStruct(shape, x.dtype)],
        dma_sems(n, n_mod * n) + [pltpu.SemaphoreType.DMA],
    )[0]


def reduce_kernel(axis, count, block, *refs):
    xs, outs = refs[:count], refs[count : 2 * count]
    greet((axis, "mod"))
    add_up(axis, count, block, xs, outs, *refs[2 * count :])


def add_up(axis, count, block, xs, outs, *refs):
    me, n = lax.axis_index(axis), lax.axis_size(axis)
    m, n_mod = lax.axis_index("mod"), lax.axis_size("mod")
    near, far, land = (refs[i * count : (1 + i) * count] for i in range(3))
    s1, r1, s2, r2 = refs[3 * count :]
    order = list(range(1, n)) + [0]
    swaps, copies = {}, []
    for step in order:
        peer = lax.rem(me + step, n)
        for which in range(count):
            for other in range(1, n_mod):
                partner = lax.rem(m + other, n_mod)
                slot = ((other - 1) * n + step) * count + which
                swaps[step, which, other] = send(
                    block(xs[which], partner, peer),
                    near[which].at[other - 1, step],
                    (s1, r1),
                    slot,
                    "mod",
                    partner,
                )

    def over_mod(step, which):
        total = block(xs[which], m, lax.rem(me + step, n))[...].astype(f32)
        for other in range(1, n_mod):
            swaps[step, which, other].wait_recv()
            total += near[which][other - 1, step].astype(f32)
        return total

    for step in range(1, n):
        for which in range(count):
            far[which][step] = over_mod(step, which).astype(bf16)
            copies.append(
                send(
                    far[which].at[step],
                    land[which].at[step],
                    (s2, r2),
                    step * count + which,
                    axis,
                    lax.rem(me + step, n),
                )
            )
    for which in range(count):
        outs[which][...] = over_mod(0, which)
    for index, copy in enumerate(copies):
        copy.wait_recv()
        step, which = 1 + index // count, index % count
        outs[which][...] += land[which][step].astype(f32)
    for copy in copies:
        copy.wait_send()
    for copy in swaps.values():
        copy.wait_send()


def add_up_scratch(axis, block_shapes):
    n_mod, n, count = lax.axis_size("mod"), lax.axis_size(axis), len(block_shapes)
    slots = [pltpu.VMEM((n_mod - 1, n) + shape, bf16) for shape in block_shapes]
    lines = [pltpu.VMEM((n,) + shape, bf16) for shape in block_shapes]
    return slots + lines + lines + dma_sems(n_mod * n * count, n * count)


def reduce(xs, axis, block, block_shapes, call_id):
    count = len(xs)
    return communicate(
        functools.partial(reduce_kernel, axis, count, block),
        call_id,
        f"reduce_{call_id}_{axis}",
        xs,
        [jax.ShapeDtypeStruct(shape, f32) for shape in block_shapes],
        add_up_scratch(axis, block_shapes),
    )


def block_of_ctx(ref, j, i):
    return ref.at[:, j, i]


def renew_kernel(part, x_ref, own_ref, sum_ref, o_ref, message, *refs):
    s1, r1, s2, r2, own_sem = refs[-5:]
    greet(("ctx", "mod"))
    add_up("ctx", 1, block_of_ctx, (x_ref,), (sum_ref,), *refs[:-5])
    residual = sum_ref[...] + own_ref[:, :, :part].astype(f32)
    sum_ref[...] = residual
    message[:, :, :part] = residual.astype(bf16)
    squares = jnp.sum(residual * residual, axis=-1, keepdims=True)
    high, low = two_parts(squares)
    lane = lax.broadcasted_iota(jnp.int32, squares.shape[:2] + (LANES,), 2)
    tags = jnp.where(lane == 0, high.astype(f32), jnp.where(lane == 1, low.astype(f32), 0.0))
    message[:, :, part:] = tags.astype(bf16)
    spread("ctx", message, lambda j, i: block_of_ctx(o_ref, j, i), (s1, r1), (s2, r2), own_sem)


def renew(product, own_block, call_id):
    n_dp, n_mod, n_ctx, rows, part = product.shape
    return communicate(
        functools.partial(renew_kernel, part),
        call_id,
        "renew",
        (product, own_block),
        [
            jax.ShapeDtypeStruct((n_dp, rows, part), f32),
            jax.ShapeDtypeStruct((n_dp, n_mod, n_ctx, rows, part + LANES), bf16),
        ],
        [pltpu.VMEM((n_dp, rows, part + LANES), bf16)]
        + add_up_scratch("ctx", [(n_dp, rows, part)])
        + dma_sems(n_ctx, n_mod * n_ctx)
        + [pltpu.SemaphoreType.DMA],
    )


def leave_kernel(part, x_ref, residual_ref, o_ref, total, message, *refs):
    s0, r0, own_sem = refs[-3:]
    greet(("ctx", "mod", "dp"))
    add_up("ctx", 1, block_of_ctx, (x_ref,), (total,), *refs[:-3])
    message[...] = (total[...] + residual_ref[...]).astype(bf16)

    def share(i):
        return o_ref.at[:, pl.ds(pl.multiple_of(i * part, part), part)]

    swap_all("dp", lambda i: message.at[i], share, (s0, r0), own_sem)


def leave(product, residual, call_id):
    n_dp, n_mod, n_ctx, rows, part = product.shape
    return communicate(
        functools.partial(leave_kernel, part),
        call_id,
        "leave",
        (product, residual),
        [jax.ShapeDtypeStruct((rows, n_dp * part), bf16)],
        [pltpu.VMEM((n_dp, rows, part), f32), pltpu.VMEM((n_dp, rows, part), bf16)]
        + add_up_scratch("ctx", [(n_dp, rows, part)])
        + dma_sems(n_dp)
        + [pltpu.SemaphoreType.DMA],
    )[0]


def attend_kernel(group, sets, rows, chunk, first_free, at_ref, q_ref, k_ref, v_ref, m_ref, o_ref, acc, total):
    step = pl.program_id(0)
    wide_head = group * HD

    @pl.when(step == 0)
    def _():
        acc[...] = jnp.zeros_like(acc)
        total[...] = jnp.zeros_like(total)

    over_width = (((1,), (1,)), ((), ()))
    of_head = lax.broadcasted_iota(jnp.int32, (8 * group, wide_head), 0) // 8
    in_head = lax.broadcasted_iota(jnp.int32, (8 * group, wide_head), 1) // HD
    ones = jnp.where(of_head == in_head, 1.0, 0.0).astype(bf16)

    def add_chunk(masked):
        is_first = m_ref[...] == 0
        for one in range(sets):
            cut = slice(one * wide_head, (one + 1) * wide_head)
            keys = k_ref[:, cut]
            both = lax.dot_general(q_ref[one], keys, over_width, preferred_element_type=f32)
            wide = keys.astype(f32)
            squares = lax.dot_general(
                ones, (wide * wide).astype(bf16), over_width, preferred_element_type=f32
            )
            inverse = lax.rsqrt(squares * (1.0 / HD) + epsilon)
            parts = []
            for h in range(group):
                at = 2 * h * rows
                scores = jnp.where(is_first, both[at : at + rows], both[at + rows : at + 2 * rows])
                probs = jnp.exp(scores * inverse[8 * h : 8 * h + 1])
                if masked:
                    key_pos = step * chunk + lax.broadcasted_iota(jnp.int32, (rows, chunk), 1)
                    row_pos = lax.broadcasted_iota(jnp.int32, (rows, chunk), 0)
                    probs = jnp.where(key_pos <= first_free + at_ref[1] + row_pos, probs, 0.0)
                total[one * group + h] += jnp.sum(probs, axis=1, keepdims=True)
                parts.append(probs.astype(bf16))
            acc[one] += jnp.dot(
                jnp.concatenate(parts, axis=0), v_ref[:, cut], preferred_element_type=f32
            )

    has_free = (step + 1) * chunk > first_free

    @pl.when(has_free)
    def _():
        add_chunk(True)

    @pl.when(jnp.logical_not(has_free))
    def _():
        add_chunk(False)

    @pl.when(step == pl.num_programs(0) - 1)
    def _():
        for head in range(sets * group):
            one, h = head // group, head % group
            summed = acc[one, h * rows : (h + 1) * rows, h * HD : (h + 1) * HD]
            o_ref[:, head * HD : (head + 1) * HD] = (summed / total[head]).astype(bf16)


def attend(queries, key_cache, value_cache, key_modality, column, row_start, slab_len):
    heads, double, _ = queries.shape
    rows = double // 2
    cache_len = key_cache.shape[0]
    chunk = min(1024, cache_len)
    width = heads * HD
    group = 2 if heads % 2 == 0 else 1
    sets = heads // group
    apart = jnp.eye(group, dtype=bf16)[None, :, None, :, None]
    queries = queries.reshape(sets, group, double, 1, HD) * apart
    queries = queries.reshape(sets, group * double, group * HD)
    where_at = jnp.stack([column, row_start]).astype(jnp.int32)
    return pl.pallas_call(
        functools.partial(attend_kernel, group, sets, rows, chunk, cache_len - slab_len),
        out_shape=jax.ShapeDtypeStruct((rows, width), bf16),
        grid_spec=pltpu.PrefetchScalarGridSpec(
            num_scalar_prefetch=1,
            grid=(cache_len // chunk,),
            in_specs=[
                pl.BlockSpec((sets, group * double, group * HD), lambda j, at: (0, 0, 0)),
                pl.BlockSpec((chunk, width), lambda j, at: (j, at[0])),
                pl.BlockSpec((chunk, width), lambda j, at: (j, at[0])),
                pl.BlockSpec((1, chunk), lambda j, at: (0, j)),
            ],
            out_specs=pl.BlockSpec((rows, width), lambda j, at: (0, 0)),
            scratch_shapes=[
                pltpu.VMEM((sets, group * rows, group * HD), f32),
                pltpu.VMEM((heads, rows, 1), f32),
            ],
        ),
        compiler_params=pltpu.CompilerParams(dimension_semantics=("arbitrary",)),
        name="attend",
    )(where_at, queries, key_cache, value_cache, key_modality)


def two_parts(values):
    high = values.astype(bf16)
    return high, (values - high.astype(f32)).astype(bf16)


def beside(values, columns):
    extra = jnp.stack([c.astype(bf16) for c in columns], axis=-1)
    pad = [(0, 0)] * (extra.ndim - 1) + [(0, LANES - extra.shape[-1])]
    return jnp.concatenate([values.astype(bf16), jnp.pad(extra, pad)], axis=-1)


def per_device(
    hidden_in,
    query_modality,
    key_cache,
    value_cache,
    key_modality,
    norm_attn,
    query_weight,
    query_gain,
    key_gain,
    out_weight,
    norm_ffn,
    gate_weight,
    up_weight,
    down_weight,
):
    m = lax.axis_index("mod")
    d = lax.axis_index("dp")
    n_mod, n_ctx, n_dp = lax.axis_size("mod"), lax.axis_size("ctx"), lax.axis_size("dp")
    rows, model = hidden_in.shape[1:]
    part = model // n_dp
    width = query_weight.shape[2]
    hidden_units = gate_weight.shape[2]
    heads = width // HD
    slab_len = n_mod * n_ctx * rows
    by_heads = heads % n_mod == 0

    hidden = hidden_in[0]
    wide = hidden.astype(f32)
    inverse = lax.rsqrt(jnp.mean(wide * wide, axis=-1) + epsilon)
    sent = jnp.broadcast_to(
        beside(jnp.zeros((rows, 0), bf16), (query_modality[0], *two_parts(inverse)))[None],
        (n_dp, rows, LANES),
    )
    pieces = hidden.reshape(rows, n_dp, part).transpose(1, 0, 2)
    own_block, slab = enter(jnp.concatenate([pieces, sent], axis=-1), 0)
    tags = slab[..., part : part + 3].astype(f32)
    ids = tags[..., 0]
    is_mine = ids == m.astype(f32)

    gain = lax.dynamic_slice_in_dim(norm_attn[0], d * part, part)
    row_inverse = (tags[..., 1] + tags[..., 2])[..., None]
    normed = jnp.where(
        is_mine[..., None], slab[..., :part].astype(f32) * row_inverse * gain, 0.0
    ).astype(bf16)
    tokens = n_dp * slab_len
    projected = jnp.dot(
        normed.reshape(tokens, part), query_weight[0], preferred_element_type=f32
    ).astype(bf16)
    gains = jnp.stack(two_parts(query_gain[0]))
    gains = jnp.where(jnp.arange(n_mod)[:, None, None] == m, gains[None], jnp.zeros_like(gains)[None])
    gains = jnp.pad(gains.reshape(2 * n_mod, width), ((0, 16 - 2 * n_mod), (0, 0)))
    gains = jnp.where(d == 0, gains, jnp.zeros_like(gains))
    split_width = width // n_mod if by_heads else width
    blocks = n_ctx * n_mod if by_heads else n_ctx
    count = blocks * rows
    if by_heads:
        to_sum = jnp.concatenate(
            [
                projected.reshape(n_dp, count, width),
                jnp.broadcast_to(gains[None], (n_dp, 16, width)),
            ],
            axis=1,
        )
        to_sum = to_sum.reshape(n_dp, count + 16, n_mod, split_width).transpose(0, 2, 1, 3)
    else:
        to_sum = jnp.concatenate(
            [
                projected.reshape(n_dp, n_mod, count, width),
                jnp.broadcast_to(gains[None, None], (n_dp, n_mod, 16, width)),
            ],
            axis=2,
        )
    (summed,) = reduce(
        (to_sum,), "dp", lambda ref, j, i: ref.at[i, j], [(count + 16, split_width)], 1
    )
    projected = summed[:count]
    both_gains = summed[count : count + 2 * n_mod : 2] + summed[count + 1 : count + 2 * n_mod : 2]
    split_heads = split_width // HD
    own_ids = lax.dynamic_index_in_dim(ids, d, 0, keepdims=False)
    if by_heads:
        own_ids = own_ids.reshape(count)
        column, row_start = m, jnp.int32(0)
        key_gains = lax.dynamic_slice_in_dim(key_gain, m * split_width, split_width, 1)
    else:
        own_ids = lax.dynamic_index_in_dim(own_ids, m, 0, keepdims=False).reshape(count)
        column, row_start = jnp.int32(0), m * count
        key_gains = key_gain
    token_gain = jnp.where(own_ids[:, None] == 0, both_gains[0][None], both_gains[1][None])
    by_head = projected.reshape(count, split_heads, HD)
    by_head = by_head * lax.rsqrt(
        jnp.mean(by_head * by_head, axis=-1, keepdims=True) + epsilon
    )
    by_head = by_head * token_gain.reshape(count, split_heads, HD) * (1.0 / math.sqrt(HD))
    queries = by_head[None] * key_gains.reshape(2, 1, split_heads, HD)
    queries = (
        queries.astype(bf16).transpose(2, 0, 1, 3).reshape(split_heads, 2 * count, HD)
    )
    head_out = attend(
        queries, key_cache[0], value_cache[0], key_modality, column, row_start, slab_len
    )

    if by_heads:
        shared = gather(
            head_out,
            "dp",
            (n_dp, count, width),
            lambda ref, j, i: ref.at[i, :, pl.ds(pl.multiple_of(j * split_width, LANES), split_width)],
            2,
        )
    else:
        shared = gather(
            head_out, "dp", (n_dp, n_mod, count, width), lambda ref, j, i: ref.at[i, j], 2
        )

    def own_product(values, weight):
        values = values.reshape(tokens, values.shape[-1])
        masked = jnp.where(is_mine.reshape(tokens, 1), values, jnp.zeros_like(values))
        product = jnp.dot(masked, weight, preferred_element_type=f32).astype(bf16)
        return product.reshape(n_dp, n_mod, n_ctx, rows, part)

    residual, slab = renew(own_product(shared, out_weight[0]), own_block, 3)

    gain = lax.dynamic_slice_in_dim(norm_ffn[0], d * part, part)
    scaled = jnp.where(is_mine[..., None], slab[..., :part].astype(f32) * gain, 0.0)
    scaled = scaled.astype(bf16).reshape(tokens, part)
    by_block = (n_dp, n_mod, n_ctx * rows)
    gate = jnp.dot(scaled, gate_weight[0], preferred_element_type=f32).astype(bf16)
    up = jnp.dot(scaled, up_weight[0], preferred_element_type=f32).astype(bf16)
    squares = jnp.where(is_mine[..., None], slab[..., part:], jnp.zeros_like(slab[..., part:]))
    gate, up, squares = reduce(
        (
            gate.reshape(*by_block, hidden_units),
            up.reshape(*by_block, hidden_units),
            squares.reshape(*by_block, LANES),
        ),
        "dp",
        lambda ref, j, i: ref.at[i, j],
        [(n_ctx * rows, hidden_units)] * 2 + [(n_ctx * rows, LANES)],
        5,
    )
    inverse = lax.rsqrt((squares[:, :1] + squares[:, 1:2]) * (1.0 / model) + epsilon)
    activated = (jax.nn.silu(gate * inverse) * (up * inverse)).astype(bf16)
    shared = gather(
        activated, "dp", (*by_block, hidden_units), lambda ref, j, i: ref.at[i, j], 6
    )
    return leave(own_product(shared, down_weight[0]), residual, 7)[None]


def solution(mesh):
    placed = (
        P("dp", ("mod", "ctx"), None),
        P("dp", ("mod", "ctx")),
        P("dp", None, "ctx"),
        P("dp", None, "ctx"),
        P("dp", None),
        P("mod", None),
        P("mod", "dp", "ctx"),
        P("mod", "ctx"),
        P(None, "ctx"),
        P("mod", "ctx", "dp"),
        P("mod", None),
        P("mod", "dp", "ctx"),
        P("mod", "dp", "ctx"),
        P("mod", "ctx", "dp"),
    )
    return jax.shard_map(
        per_device,
        mesh=mesh,
        in_specs=placed,
        out_specs=P("dp", ("mod", "ctx"), None),
        check_vma=False,
    )
```

```python
import functools
import math

import jax
import jax.numpy as jnp
from jax import lax
from jax.experimental import pallas as pl
from jax.experimental.pallas import tpu as pltpu
from jax.sharding import PartitionSpec as P

HD = 128
LANES = 128

epsilon = 1e-05
bf16 = jnp.bfloat16
f32 = jnp.float32


def greet(axes):
    barrier = pltpu.get_barrier_semaphore()
    count = 0
    for axis in axes:
        me, n = lax.axis_index(axis), lax.axis_size(axis)
        for step in range(1, n):
            pl.semaphore_signal(
                barrier,
                inc=1,
                device_id={axis: lax.rem(me + step, n)},
                device_id_type=pl.DeviceIdType.MESH,
            )
        count += n - 1
    pl.semaphore_wait(barrier, count)


def send(source, target, sems, slot, axis, peer):
    copy = pltpu.make_async_remote_copy(
        src_ref=source,
        dst_ref=target,
        send_sem=sems[0].at[slot],
        recv_sem=sems[1].at[slot],
        device_id={axis: peer},
        device_id_type=pl.DeviceIdType.MESH,
    )
    copy.start()
    return copy


def copy_here(source, target, sem):
    copy = pltpu.make_async_copy(source, target, sem)
    copy.start()
    copy.wait()


def swap_all(axis, source_of, target_of, sems, own_sem):
    me, n = lax.axis_index(axis), lax.axis_size(axis)
    copies = []
    for step in range(1, n):
        peer = lax.rem(me + step, n)
        copies.append(send(source_of(peer), target_of(me), sems, step, axis, peer))
    copy_here(source_of(me), target_of(me), own_sem)
    for copy in copies:
        copy.wait()


def spread(axis, source, place, sems, relay_sems, own_sem):
    me, n = lax.axis_index(axis), lax.axis_size(axis)
    m, n_mod = lax.axis_index("mod"), lax.axis_size("mod")
    copies, relays = [], []
    for step in range(1, n):
        peer = lax.rem(me + step, n)
        copies.append(send(source, place(m, me), sems, step, axis, peer))

    def relay(block, origin, step):
        for other in range(1, n_mod):
            partner = lax.rem(m + other, n_mod)
            slot = (other - 1) * n + step
            relays.append(send(block, place(m, origin), relay_sems, slot, "mod", partner))

    relay(source, me, 0)
    copy_here(source, place(m, me), own_sem)
    for step in range(1, n):
        copies[step - 1].wait_recv()
        origin = lax.rem(me + n - step, n)
        relay(place(m, origin), origin, step)
    for copy in copies:
        copy.wait_send()
    for copy in relays:
        copy.wait()


def dma_sems(*counts):
    return [pltpu.SemaphoreType.DMA((count,)) for count in counts for _ in range(2)]


def communicate(kernel, call_id, name, operands, outs, scratch):
    whole = pl.BlockSpec(memory_space=pltpu.VMEM)
    return pl.pallas_call(
        kernel,
        out_shape=outs,
        in_specs=[whole] * len(operands),
        out_specs=[whole] * len(outs),
        scratch_shapes=scratch,
        compiler_params=pltpu.CompilerParams(
            collective_id=call_id, has_side_effects=True, vmem_limit_bytes=60 * 2**20
        ),
        name=name,
    )(*operands)


def enter_kernel(x_ref, block_ref, o_ref, s0, r0, s1, r1, s2, r2, own_sem):
    greet(("dp", "ctx", "mod"))
    swap_all("dp", lambda i: x_ref.at[i], lambda i: block_ref.at[i], (s0, r0), own_sem)
    spread("ctx", block_ref, lambda j, i: o_ref.at[:, j, i], (s1, r1), (s2, r2), own_sem)


def enter(x, call_id):
    n_dp, rows, cols = x.shape
    n_mod, n_ctx = lax.axis_size("mod"), lax.axis_size("ctx")
    return communicate(
        enter_kernel,
        call_id,
        "enter",
        (x,),
        [
            jax.ShapeDtypeStruct(x.shape, x.dtype),
            jax.ShapeDtypeStruct((n_dp, n_mod, n_ctx, rows, cols), x.dtype),
        ],
        dma_sems(n_dp, n_ctx, n_mod * n_ctx) + [pltpu.SemaphoreType.DMA],
    )


def gather(x, axis, shape, place, call_id):
    n_mod, n = lax.axis_size("mod"), lax.axis_size(axis)

    def kernel(x_ref, o_ref, s1, r1, s2, r2, own_sem):
        greet((axis, "mod"))
        spread(axis, x_ref, lambda j, i: place(o_ref, j, i), (s1, r1), (s2, r2), own_sem)

    return communicate(
        kernel,
        call_id,
        f"gather_{call_id}_{axis}",
        (x,),
        [jax.ShapeDtypeStruct(shape, x.dtype)],
        dma_sems(n, n_mod * n) + [pltpu.SemaphoreType.DMA],
    )[0]


def reduce_kernel(axis, count, block, *refs):
    xs, outs = refs[:count], refs[count : 2 * count]
    greet((axis, "mod"))
    add_up(axis, count, block, xs, outs, *refs[2 * count :])


def add_up(axis, count, block, xs, outs, *refs):
    me, n = lax.axis_index(axis), lax.axis_size(axis)
    m, n_mod = lax.axis_index("mod"), lax.axis_size("mod")
    near, far, land = (refs[i * count : (1 + i) * count] for i in range(3))
    s1, r1, s2, r2 = refs[3 * count :]
    order = list(range(1, n)) + [0]
    swaps, copies = {}, []
    for step in order:
        peer = lax.rem(me + step, n)
        for which in range(count):
            for other in range(1, n_mod):
                partner = lax.rem(m + other, n_mod)
                slot = ((other - 1) * n + step) * count + which
                swaps[step, which, other] = send(
                    block(xs[which], partner, peer),
                    near[which].at[other - 1, step],
                    (s1, r1),
                    slot,
                    "mod",
                    partner,
                )

    def over_mod(step, which):
        total = block(xs[which], m, lax.rem(me + step, n))[...].astype(f32)
        for other in range(1, n_mod):
            swaps[step, which, other].wait_recv()
            total += near[which][other - 1, step].astype(f32)
        return total

    for step in range(1, n):
        for which in range(count):
            far[which][step] = over_mod(step, which).astype(bf16)
            copies.append(
                send(
                    far[which].at[step],
                    land[which].at[step],
                    (s2, r2),
                    step * count + which,
                    axis,
                    lax.rem(me + step, n),
                )
            )
    for which in range(count):
        outs[which][...] = over_mod(0, which)
    for index, copy in enumerate(copies):
        copy.wait_recv()
        step, which = 1 + index // count, index % count
        outs[which][...] += land[which][step].astype(f32)
    for copy in copies:
        copy.wait_send()
    for copy in swaps.values():
        copy.wait_send()


def add_up_scratch(axis, block_shapes):
    n_mod, n, count = lax.axis_size("mod"), lax.axis_size(axis), len(block_shapes)
    slots = [pltpu.VMEM((n_mod - 1, n) + shape, bf16) for shape in block_shapes]
    lines = [pltpu.VMEM((n,) + shape, bf16) for shape in block_shapes]
    return slots + lines + lines + dma_sems(n_mod * n * count, n * count)


def reduce(xs, axis, block, block_shapes, call_id):
    count = len(xs)
    return communicate(
        functools.partial(reduce_kernel, axis, count, block),
        call_id,
        f"reduce_{call_id}_{axis}",
        xs,
        [jax.ShapeDtypeStruct(shape, f32) for shape in block_shapes],
        add_up_scratch(axis, block_shapes),
    )


def block_of_ctx(ref, j, i):
    return ref.at[:, j, i]


def renew_kernel(part, x_ref, own_ref, sum_ref, o_ref, message, *refs):
    s1, r1, s2, r2, own_sem = refs[-5:]
    greet(("ctx", "mod"))
    add_up("ctx", 1, block_of_ctx, (x_ref,), (sum_ref,), *refs[:-5])
    residual = sum_ref[...] + own_ref[:, :, :part].astype(f32)
    sum_ref[...] = residual
    message[:, :, :part] = residual.astype(bf16)
    squares = jnp.sum(residual * residual, axis=-1, keepdims=True)
    high, low = two_parts(squares)
    lane = lax.broadcasted_iota(jnp.int32, squares.shape[:2] + (LANES,), 2)
    tags = jnp.where(lane == 0, high.astype(f32), jnp.where(lane == 1, low.astype(f32), 0.0))
    message[:, :, part:] = tags.astype(bf16)
    spread("ctx", message, lambda j, i: block_of_ctx(o_ref, j, i), (s1, r1), (s2, r2), own_sem)


def renew(product, own_block, call_id):
    n_dp, n_mod, n_ctx, rows, part = product.shape
    return communicate(
        functools.partial(renew_kernel, part),
        call_id,
        "renew",
        (product, own_block),
        [
            jax.ShapeDtypeStruct((n_dp, rows, part), f32),
            jax.ShapeDtypeStruct((n_dp, n_mod, n_ctx, rows, part + LANES), bf16),
        ],
        [pltpu.VMEM((n_dp, rows, part + LANES), bf16)]
        + add_up_scratch("ctx", [(n_dp, rows, part)])
        + dma_sems(n_ctx, n_mod * n_ctx)
        + [pltpu.SemaphoreType.DMA],
    )


def block_of_dp(ref, j, i):
    return ref.at[i, j]


def activate_kernel(model, gate_ref, up_ref, tag_ref, o_ref, gate_sum, up_sum, tag_sum, message, *refs):
    s1, r1, s2, r2, own_sem = refs[-5:]
    greet(("dp", "mod"))
    sums = (gate_sum, up_sum, tag_sum)
    add_up("dp", 3, block_of_dp, (gate_ref, up_ref, tag_ref), sums, *refs[:-5])
    squares = tag_sum[:, :1] + tag_sum[:, 1:2]
    inverse = lax.rsqrt(squares * (1.0 / model) + epsilon)
    gate = gate_sum[...] * inverse
    message[...] = (gate / (1.0 + jnp.exp(-gate)) * (up_sum[...] * inverse)).astype(bf16)
    spread("dp", message, lambda j, i: block_of_dp(o_ref, j, i), (s1, r1), (s2, r2), own_sem)


def activate(gate, up, tags, model, call_id):
    n_dp, n_mod, count, hidden_units = gate.shape
    shapes = [(count, hidden_units)] * 2 + [(count, LANES)]
    return communicate(
        functools.partial(activate_kernel, model),
        call_id,
        "activate",
        (gate, up, tags),
        [jax.ShapeDtypeStruct(gate.shape, bf16)],
        [pltpu.VMEM(shape, f32) for shape in shapes]
        + [pltpu.VMEM((count, hidden_units), bf16)]
        + add_up_scratch("dp", shapes)
        + dma_sems(n_dp, n_mod * n_dp)
        + [pltpu.SemaphoreType.DMA],
    )[0]


def expand_kernel(x_ref, gate_ref, up_ref, gate_out, up_out):
    x = x_ref[...]
    gate_out[...] = jnp.dot(x, gate_ref[...], preferred_element_type=f32).astype(bf16)
    up_out[...] = jnp.dot(x, up_ref[...], preferred_element_type=f32).astype(bf16)


def expand(x, gate_weight, up_weight):
    tokens, part = x.shape
    hidden_units = gate_weight.shape[1]
    tile = min(512, hidden_units)
    weight = pl.BlockSpec((part, tile), lambda j: (0, j))
    product = pl.BlockSpec((tokens, tile), lambda j: (0, j))
    out = jax.ShapeDtypeStruct((tokens, hidden_units), bf16)
    return pl.pallas_call(
        expand_kernel,
        grid=(pl.cdiv(hidden_units, tile),),
        in_specs=[pl.BlockSpec((tokens, part), lambda j: (0, 0)), weight, weight],
        out_specs=[product, product],
        out_shape=[out, out],
        compiler_params=pltpu.CompilerParams(
            dimension_semantics=("arbitrary",), vmem_limit_bytes=60 * 2**20
        ),
        name="expand",
    )(x, gate_weight, up_weight)


def leave_kernel(part, x_ref, residual_ref, o_ref, total, message, *refs):
    s0, r0, own_sem = refs[-3:]
    greet(("ctx", "mod", "dp"))
    add_up("ctx", 1, block_of_ctx, (x_ref,), (total,), *refs[:-3])
    message[...] = (total[...] + residual_ref[...]).astype(bf16)

    def share(i):
        return o_ref.at[:, pl.ds(pl.multiple_of(i * part, part), part)]

    swap_all("dp", lambda i: message.at[i], share, (s0, r0), own_sem)


def leave(product, residual, call_id):
    n_dp, n_mod, n_ctx, rows, part = product.shape
    return communicate(
        functools.partial(leave_kernel, part),
        call_id,
        "leave",
        (product, residual),
        [jax.ShapeDtypeStruct((rows, n_dp * part), bf16)],
        [pltpu.VMEM((n_dp, rows, part), f32), pltpu.VMEM((n_dp, rows, part), bf16)]
        + add_up_scratch("ctx", [(n_dp, rows, part)])
        + dma_sems(n_dp)
        + [pltpu.SemaphoreType.DMA],
    )[0]


def attend_kernel(group, sets, rows, chunk, first_free, at_ref, q_ref, k_ref, v_ref, m_ref, o_ref, acc, total):
    step = pl.program_id(0)
    wide_head = group * HD

    @pl.when(step == 0)
    def _():
        acc[...] = jnp.zeros_like(acc)
        total[...] = jnp.zeros_like(total)

    over_width = (((1,), (1,)), ((), ()))
    of_head = lax.broadcasted_iota(jnp.int32, (8 * group, wide_head), 0) // 8
    in_head = lax.broadcasted_iota(jnp.int32, (8 * group, wide_head), 1) // HD
    ones = jnp.where(of_head == in_head, 1.0, 0.0).astype(bf16)

    def add_chunk(masked):
        is_first = m_ref[...] == 0
        for one in range(sets):
            cut = slice(one * wide_head, (one + 1) * wide_head)
            keys = k_ref[:, cut]
            both = lax.dot_general(q_ref[one], keys, over_width, preferred_element_type=f32)
            wide = keys.astype(f32)
            squares = lax.dot_general(
                ones, (wide * wide).astype(bf16), over_width, preferred_element_type=f32
            )
            inverse = lax.rsqrt(squares * (1.0 / HD) + epsilon)
            parts = []
            for h in range(group):
                at = 2 * h * rows
                scores = jnp.where(is_first, both[at : at + rows], both[at + rows : at + 2 * rows])
                probs = jnp.exp(scores * inverse[8 * h : 8 * h + 1])
                if masked:
                    key_pos = step * chunk + lax.broadcasted_iota(jnp.int32, (rows, chunk), 1)
                    row_pos = lax.broadcasted_iota(jnp.int32, (rows, chunk), 0)
                    probs = jnp.where(key_pos <= first_free + at_ref[1] + row_pos, probs, 0.0)
                total[one * group + h] += jnp.sum(probs, axis=1, keepdims=True)
                parts.append(probs.astype(bf16))
            acc[one] += jnp.dot(
                jnp.concatenate(parts, axis=0), v_ref[:, cut], preferred_element_type=f32
            )

    has_free = (step + 1) * chunk > first_free

    @pl.when(has_free)
    def _():
        add_chunk(True)

    @pl.when(jnp.logical_not(has_free))
    def _():
        add_chunk(False)

    @pl.when(step == pl.num_programs(0) - 1)
    def _():
        for head in range(sets * group):
            one, h = head // group, head % group
            summed = acc[one, h * rows : (h + 1) * rows, h * HD : (h + 1) * HD]
            o_ref[:, head * HD : (head + 1) * HD] = (summed / total[head]).astype(bf16)


def attend(queries, key_cache, value_cache, key_modality, column, row_start, slab_len):
    heads, double, _ = queries.shape
    rows = double // 2
    cache_len = key_cache.shape[0]
    chunk = min(1024, cache_len)
    width = heads * HD
    group = 2 if heads % 2 == 0 else 1
    sets = heads // group
    apart = jnp.eye(group, dtype=bf16)[None, :, None, :, None]
    queries = queries.reshape(sets, group, double, 1, HD) * apart
    queries = queries.reshape(sets, group * double, group * HD)
    where_at = jnp.stack([column, row_start]).astype(jnp.int32)
    return pl.pallas_call(
        functools.partial(attend_kernel, group, sets, rows, chunk, cache_len - slab_len),
        out_shape=jax.ShapeDtypeStruct((rows, width), bf16),
        grid_spec=pltpu.PrefetchScalarGridSpec(
            num_scalar_prefetch=1,
            grid=(cache_len // chunk,),
            in_specs=[
                pl.BlockSpec((sets, group * double, group * HD), lambda j, at: (0, 0, 0)),
                pl.BlockSpec((chunk, width), lambda j, at: (j, at[0])),
                pl.BlockSpec((chunk, width), lambda j, at: (j, at[0])),
                pl.BlockSpec((1, chunk), lambda j, at: (0, j)),
            ],
            out_specs=pl.BlockSpec((rows, width), lambda j, at: (0, 0)),
            scratch_shapes=[
                pltpu.VMEM((sets, group * rows, group * HD), f32),
                pltpu.VMEM((heads, rows, 1), f32),
            ],
        ),
        compiler_params=pltpu.CompilerParams(dimension_semantics=("arbitrary",)),
        name="attend",
    )(where_at, queries, key_cache, value_cache, key_modality)


def two_parts(values):
    high = values.astype(bf16)
    return high, (values - high.astype(f32)).astype(bf16)


def beside(values, columns):
    extra = jnp.stack([c.astype(bf16) for c in columns], axis=-1)
    pad = [(0, 0)] * (extra.ndim - 1) + [(0, LANES - extra.shape[-1])]
    return jnp.concatenate([values.astype(bf16), jnp.pad(extra, pad)], axis=-1)


def per_device(
    hidden_in,
    query_modality,
    key_cache,
    value_cache,
    key_modality,
    norm_attn,
    query_weight,
    query_gain,
    key_gain,
    out_weight,
    norm_ffn,
    gate_weight,
    up_weight,
    down_weight,
):
    m = lax.axis_index("mod")
    d = lax.axis_index("dp")
    n_mod, n_ctx, n_dp = lax.axis_size("mod"), lax.axis_size("ctx"), lax.axis_size("dp")
    rows, model = hidden_in.shape[1:]
    part = model // n_dp
    width = query_weight.shape[2]
    hidden_units = gate_weight.shape[2]
    heads = width // HD
    slab_len = n_mod * n_ctx * rows
    by_heads = heads % n_mod == 0

    hidden = hidden_in[0]
    wide = hidden.astype(f32)
    inverse = lax.rsqrt(jnp.mean(wide * wide, axis=-1) + epsilon)
    sent = jnp.broadcast_to(
        beside(jnp.zeros((rows, 0), bf16), (query_modality[0], *two_parts(inverse)))[None],
        (n_dp, rows, LANES),
    )
    pieces = hidden.reshape(rows, n_dp, part).transpose(1, 0, 2)
    own_block, slab = enter(jnp.concatenate([pieces, sent], axis=-1), 0)
    tags = slab[..., part : part + 3].astype(f32)
    ids = tags[..., 0]
    is_mine = ids == m.astype(f32)

    gain = lax.dynamic_slice_in_dim(norm_attn[0], d * part, part)
    row_inverse = (tags[..., 1] + tags[..., 2])[..., None]
    normed = jnp.where(
        is_mine[..., None], slab[..., :part].astype(f32) * row_inverse * gain, 0.0
    ).astype(bf16)
    tokens = n_dp * slab_len
    projected = jnp.dot(
        normed.reshape(tokens, part), query_weight[0], preferred_element_type=f32
    ).astype(bf16)
    gains = jnp.stack(two_parts(query_gain[0]))
    gains = jnp.where(jnp.arange(n_mod)[:, None, None] == m, gains[None], jnp.zeros_like(gains)[None])
    gains = jnp.pad(gains.reshape(2 * n_mod, width), ((0, 16 - 2 * n_mod), (0, 0)))
    gains = jnp.where(d == 0, gains, jnp.zeros_like(gains))
    split_width = width // n_mod if by_heads else width
    blocks = n_ctx * n_mod if by_heads else n_ctx
    count = blocks * rows
    if by_heads:
        to_sum = jnp.concatenate(
            [
                projected.reshape(n_dp, count, width),
                jnp.broadcast_to(gains[None], (n_dp, 16, width)),
            ],
            axis=1,
        )
        to_sum = to_sum.reshape(n_dp, count + 16, n_mod, split_width).transpose(0, 2, 1, 3)
    else:
        to_sum = jnp.concatenate(
            [
                projected.reshape(n_dp, n_mod, count, width),
                jnp.broadcast_to(gains[None, None], (n_dp, n_mod, 16, width)),
            ],
            axis=2,
        )
    (summed,) = reduce(
        (to_sum,), "dp", lambda ref, j, i: ref.at[i, j], [(count + 16, split_width)], 1
    )
    projected = summed[:count]
    both_gains = summed[count : count + 2 * n_mod : 2] + summed[count + 1 : count + 2 * n_mod : 2]
    split_heads = split_width // HD
    own_ids = lax.dynamic_index_in_dim(ids, d, 0, keepdims=False)
    if by_heads:
        own_ids = own_ids.reshape(count)
        column, row_start = m, jnp.int32(0)
        key_gains = lax.dynamic_slice_in_dim(key_gain, m * split_width, split_width, 1)
    else:
        own_ids = lax.dynamic_index_in_dim(own_ids, m, 0, keepdims=False).reshape(count)
        column, row_start = jnp.int32(0), m * count
        key_gains = key_gain
    token_gain = jnp.where(own_ids[:, None] == 0, both_gains[0][None], both_gains[1][None])
    by_head = projected.reshape(count, split_heads, HD)
    by_head = by_head * lax.rsqrt(
        jnp.mean(by_head * by_head, axis=-1, keepdims=True) + epsilon
    )
    by_head = by_head * token_gain.reshape(count, split_heads, HD) * (1.0 / math.sqrt(HD))
    queries = by_head[None] * key_gains.reshape(2, 1, split_heads, HD)
    queries = (
        queries.astype(bf16).transpose(2, 0, 1, 3).reshape(split_heads, 2 * count, HD)
    )
    head_out = attend(
        queries, key_cache[0], value_cache[0], key_modality, column, row_start, slab_len
    )

    if by_heads:
        shared = gather(
            head_out,
            "dp",
            (n_dp, count, width),
            lambda ref, j, i: ref.at[i, :, pl.ds(pl.multiple_of(j * split_width, LANES), split_width)],
            2,
        )
    else:
        shared = gather(
            head_out, "dp", (n_dp, n_mod, count, width), lambda ref, j, i: ref.at[i, j], 2
        )

    def own_product(values, weight):
        values = values.reshape(tokens, values.shape[-1])
        product = jnp.dot(values, weight, preferred_element_type=f32)
        product = jnp.where(is_mine.reshape(tokens, 1), product, 0.0).astype(bf16)
        return product.reshape(n_dp, n_mod, n_ctx, rows, part)

    residual, slab = renew(own_product(shared, out_weight[0]), own_block, 3)

    gain = lax.dynamic_slice_in_dim(norm_ffn[0], d * part, part)
    scaled = jnp.where(is_mine[..., None], slab[..., :part].astype(f32) * gain, 0.0)
    scaled = scaled.astype(bf16).reshape(tokens, part)
    by_block = (n_dp, n_mod, n_ctx * rows)
    gate, up = expand(scaled, gate_weight[0], up_weight[0])
    squares = jnp.where(is_mine[..., None], slab[..., part:], jnp.zeros_like(slab[..., part:]))
    shared = activate(
        gate.reshape(*by_block, hidden_units),
        up.reshape(*by_block, hidden_units),
        squares.reshape(*by_block, LANES),
        model,
        5,
    )
    return leave(own_product(shared, down_weight[0]), residual, 7)[None]


def solution(mesh):
    placed = (
        P("dp", ("mod", "ctx"), None),
        P("dp", ("mod", "ctx")),
        P("dp", None, "ctx"),
        P("dp", None, "ctx"),
        P("dp", None),
        P("mod", None),
        P("mod", "dp", "ctx"),
        P("mod", "ctx"),
        P(None, "ctx"),
        P("mod", "ctx", "dp"),
        P("mod", None),
        P("mod", "dp", "ctx"),
        P("mod", "dp", "ctx"),
        P("mod", "ctx", "dp"),
    )
    return jax.shard_map(
        per_device,
        mesh=mesh,
        in_specs=placed,
        out_specs=P("dp", ("mod", "ctx"), None),
        check_vma=False,
    )
```

```python
import functools
import math

import jax
import jax.numpy as jnp
from jax import lax
from jax.experimental import pallas as pl
from jax.experimental.pallas import tpu as pltpu
from jax.sharding import PartitionSpec as P

HD = 128
LANES = 128

epsilon = 1e-05
bf16 = jnp.bfloat16
f32 = jnp.float32


def greet(axes):
    barrier = pltpu.get_barrier_semaphore()
    count = 0
    for axis in axes:
        me, n = lax.axis_index(axis), lax.axis_size(axis)
        for step in range(1, n):
            pl.semaphore_signal(
                barrier,
                inc=1,
                device_id={axis: lax.rem(me + step, n)},
                device_id_type=pl.DeviceIdType.MESH,
            )
        count += n - 1
    pl.semaphore_wait(barrier, count)


def send(source, target, sems, slot, axis, peer):
    copy = pltpu.make_async_remote_copy(
        src_ref=source,
        dst_ref=target,
        send_sem=sems[0].at[slot],
        recv_sem=sems[1].at[slot],
        device_id={axis: peer},
        device_id_type=pl.DeviceIdType.MESH,
    )
    copy.start()
    return copy


def copy_here(source, target, sem):
    copy = pltpu.make_async_copy(source, target, sem)
    copy.start()
    copy.wait()


def swap_all(axis, source_of, target_of, sems, own_sem):
    me, n = lax.axis_index(axis), lax.axis_size(axis)
    copies = []
    for step in range(1, n):
        peer = lax.rem(me + step, n)
        copies.append(send(source_of(peer), target_of(me), sems, step, axis, peer))
    copy_here(source_of(me), target_of(me), own_sem)
    for copy in copies:
        copy.wait()


def spread(axis, source, place, sems, relay_sems, own_sem):
    me, n = lax.axis_index(axis), lax.axis_size(axis)
    m, n_mod = lax.axis_index("mod"), lax.axis_size("mod")
    copies, relays = [], []
    for step in range(1, n):
        peer = lax.rem(me + step, n)
        copies.append(send(source, place(m, me), sems, step, axis, peer))

    def relay(block, origin, step):
        for other in range(1, n_mod):
            partner = lax.rem(m + other, n_mod)
            slot = (other - 1) * n + step
            relays.append(send(block, place(m, origin), relay_sems, slot, "mod", partner))

    relay(source, me, 0)
    copy_here(source, place(m, me), own_sem)
    for step in range(1, n):
        copies[step - 1].wait_recv()
        origin = lax.rem(me + n - step, n)
        relay(place(m, origin), origin, step)
    for copy in copies:
        copy.wait_send()
    for copy in relays:
        copy.wait()


def dma_sems(*counts):
    return [pltpu.SemaphoreType.DMA((count,)) for count in counts for _ in range(2)]


def communicate(kernel, call_id, name, operands, outs, scratch):
    whole = pl.BlockSpec(memory_space=pltpu.VMEM)
    return pl.pallas_call(
        kernel,
        out_shape=outs,
        in_specs=[whole] * len(operands),
        out_specs=[whole] * len(outs),
        scratch_shapes=scratch,
        compiler_params=pltpu.CompilerParams(
            collective_id=call_id, has_side_effects=True, vmem_limit_bytes=60 * 2**20
        ),
        name=name,
    )(*operands)


def enter_kernel(x_ref, block_ref, o_ref, s0, r0, s1, r1, s2, r2, own_sem):
    greet(("dp", "ctx", "mod"))
    swap_all("dp", lambda i: x_ref.at[i], lambda i: block_ref.at[i], (s0, r0), own_sem)
    spread("ctx", block_ref, lambda j, i: o_ref.at[:, j, i], (s1, r1), (s2, r2), own_sem)


def enter(x, call_id):
    n_dp, rows, cols = x.shape
    n_mod, n_ctx = lax.axis_size("mod"), lax.axis_size("ctx")
    return communicate(
        enter_kernel,
        call_id,
        "enter",
        (x,),
        [
            jax.ShapeDtypeStruct(x.shape, x.dtype),
            jax.ShapeDtypeStruct((n_dp, n_mod, n_ctx, rows, cols), x.dtype),
        ],
        dma_sems(n_dp, n_ctx, n_mod * n_ctx) + [pltpu.SemaphoreType.DMA],
    )


def gather(x, axis, shape, place, call_id):
    n_mod, n = lax.axis_size("mod"), lax.axis_size(axis)

    def kernel(x_ref, o_ref, s1, r1, s2, r2, own_sem):
        greet((axis, "mod"))
        spread(axis, x_ref, lambda j, i: place(o_ref, j, i), (s1, r1), (s2, r2), own_sem)

    return communicate(
        kernel,
        call_id,
        f"gather_{call_id}_{axis}",
        (x,),
        [jax.ShapeDtypeStruct(shape, x.dtype)],
        dma_sems(n, n_mod * n) + [pltpu.SemaphoreType.DMA],
    )[0]


def reduce_kernel(axis, count, block, *refs):
    xs, outs = refs[:count], refs[count : 2 * count]
    greet((axis, "mod"))
    add_up(axis, count, block, xs, outs, *refs[2 * count :])


def add_up(axis, count, block, xs, outs, *refs):
    me, n = lax.axis_index(axis), lax.axis_size(axis)
    m, n_mod = lax.axis_index("mod"), lax.axis_size("mod")
    near, far, land = (refs[i * count : (1 + i) * count] for i in range(3))
    s1, r1, s2, r2 = refs[3 * count :]
    order = list(range(1, n)) + [0]
    swaps, copies = {}, []
    for step in order:
        peer = lax.rem(me + step, n)
        for which in range(count):
            for other in range(1, n_mod):
                partner = lax.rem(m + other, n_mod)
                slot = ((other - 1) * n + step) * count + which
                swaps[step, which, other] = send(
                    block(xs[which], partner, peer),
                    near[which].at[other - 1, step],
                    (s1, r1),
                    slot,
                    "mod",
                    partner,
                )

    def over_mod(step, which):
        total = block(xs[which], m, lax.rem(me + step, n))[...].astype(f32)
        for other in range(1, n_mod):
            swaps[step, which, other].wait_recv()
            total += near[which][other - 1, step].astype(f32)
        return total

    for step in range(1, n):
        for which in range(count):
            far[which][step] = over_mod(step, which).astype(bf16)
            copies.append(
                send(
                    far[which].at[step],
                    land[which].at[step],
                    (s2, r2),
                    step * count + which,
                    axis,
                    lax.rem(me + step, n),
                )
            )
    for which in range(count):
        outs[which][...] = over_mod(0, which)
    for index, copy in enumerate(copies):
        copy.wait_recv()
        step, which = 1 + index // count, index % count
        outs[which][...] += land[which][step].astype(f32)
    for copy in copies:
        copy.wait_send()
    for copy in swaps.values():
        copy.wait_send()


def add_up_scratch(axis, block_shapes):
    n_mod, n, count = lax.axis_size("mod"), lax.axis_size(axis), len(block_shapes)
    slots = [pltpu.VMEM((n_mod - 1, n) + shape, bf16) for shape in block_shapes]
    lines = [pltpu.VMEM((n,) + shape, bf16) for shape in block_shapes]
    return slots + lines + lines + dma_sems(n_mod * n * count, n * count)


def reduce(xs, axis, block, block_shapes, call_id):
    count = len(xs)
    return communicate(
        functools.partial(reduce_kernel, axis, count, block),
        call_id,
        f"reduce_{call_id}_{axis}",
        xs,
        [jax.ShapeDtypeStruct(shape, f32) for shape in block_shapes],
        add_up_scratch(axis, block_shapes),
    )


def block_of_ctx(ref, j, i):
    return ref.at[:, j, i]


def renew_kernel(part, x_ref, own_ref, sum_ref, o_ref, message, *refs):
    s1, r1, s2, r2, own_sem = refs[-5:]
    greet(("ctx", "mod"))
    add_up("ctx", 1, block_of_ctx, (x_ref,), (sum_ref,), *refs[:-5])
    residual = sum_ref[...] + own_ref[:, :, :part].astype(f32)
    sum_ref[...] = residual
    message[:, :, :part] = residual.astype(bf16)
    squares = jnp.sum(residual * residual, axis=-1, keepdims=True)
    high, low = two_parts(squares)
    lane = lax.broadcasted_iota(jnp.int32, squares.shape[:2] + (LANES,), 2)
    tags = jnp.where(lane == 0, high.astype(f32), jnp.where(lane == 1, low.astype(f32), 0.0))
    message[:, :, part:] = tags.astype(bf16)
    spread("ctx", message, lambda j, i: block_of_ctx(o_ref, j, i), (s1, r1), (s2, r2), own_sem)


def renew(product, own_block, call_id):
    n_dp, n_mod, n_ctx, rows, part = product.shape
    return communicate(
        functools.partial(renew_kernel, part),
        call_id,
        "renew",
        (product, own_block),
        [
            jax.ShapeDtypeStruct((n_dp, rows, part), f32),
            jax.ShapeDtypeStruct((n_dp, n_mod, n_ctx, rows, part + LANES), bf16),
        ],
        [pltpu.VMEM((n_dp, rows, part + LANES), bf16)]
        + add_up_scratch("ctx", [(n_dp, rows, part)])
        + dma_sems(n_ctx, n_mod * n_ctx)
        + [pltpu.SemaphoreType.DMA],
    )


def block_of_dp(ref, j, i):
    return ref.at[i, j]


def activate_kernel(model, gate_ref, up_ref, tag_ref, o_ref, gate_sum, up_sum, tag_sum, message, *refs):
    s1, r1, s2, r2, own_sem = refs[-5:]
    greet(("dp", "mod"))
    sums = (gate_sum, up_sum, tag_sum)
    add_up("dp", 3, block_of_dp, (gate_ref, up_ref, tag_ref), sums, *refs[:-5])
    squares = tag_sum[:, :1] + tag_sum[:, 1:2]
    inverse = lax.rsqrt(squares * (1.0 / model) + epsilon)
    gate = gate_sum[...] * inverse
    message[...] = (gate / (1.0 + jnp.exp(-gate)) * (up_sum[...] * inverse)).astype(bf16)
    spread("dp", message, lambda j, i: block_of_dp(o_ref, j, i), (s1, r1), (s2, r2), own_sem)


def activate(gate, up, tags, model, call_id):
    n_dp, n_mod, count, hidden_units = gate.shape
    shapes = [(count, hidden_units)] * 2 + [(count, LANES)]
    return communicate(
        functools.partial(activate_kernel, model),
        call_id,
        "activate",
        (gate, up, tags),
        [jax.ShapeDtypeStruct(gate.shape, bf16)],
        [pltpu.VMEM(shape, f32) for shape in shapes]
        + [pltpu.VMEM((count, hidden_units), bf16)]
        + add_up_scratch("dp", shapes)
        + dma_sems(n_dp, n_mod * n_dp)
        + [pltpu.SemaphoreType.DMA],
    )[0]


def expand_kernel(x_ref, gate_ref, up_ref, gate_out, up_out):
    x = x_ref[...]
    over_width = (((1,), (1,)), ((), ()))
    for weight, out in ((gate_ref, gate_out), (up_ref, up_out)):
        product = lax.dot_general(x, weight[...], over_width, preferred_element_type=f32)
        out[...] = product.astype(bf16)


def expand(x, gate_weight, up_weight):
    tokens, part = x.shape
    hidden_units = gate_weight.shape[0]
    tile = min(512, hidden_units)
    weight = pl.BlockSpec((tile, part), lambda j: (j, 0))
    product = pl.BlockSpec((tokens, tile), lambda j: (0, j))
    out = jax.ShapeDtypeStruct((tokens, hidden_units), bf16)
    return pl.pallas_call(
        expand_kernel,
        grid=(pl.cdiv(hidden_units, tile),),
        in_specs=[pl.BlockSpec((tokens, part), lambda j: (0, 0)), weight, weight],
        out_specs=[product, product],
        out_shape=[out, out],
        compiler_params=pltpu.CompilerParams(
            dimension_semantics=("arbitrary",), vmem_limit_bytes=60 * 2**20
        ),
        name="expand",
    )(x, gate_weight, up_weight)


def leave_kernel(part, x_ref, residual_ref, o_ref, total, message, *refs):
    s0, r0, own_sem = refs[-3:]
    greet(("ctx", "mod", "dp"))
    add_up("ctx", 1, block_of_ctx, (x_ref,), (total,), *refs[:-3])
    message[...] = (total[...] + residual_ref[...]).astype(bf16)

    def share(i):
        return o_ref.at[:, pl.ds(pl.multiple_of(i * part, part), part)]

    swap_all("dp", lambda i: message.at[i], share, (s0, r0), own_sem)


def leave(product, residual, call_id):
    n_dp, n_mod, n_ctx, rows, part = product.shape
    return communicate(
        functools.partial(leave_kernel, part),
        call_id,
        "leave",
        (product, residual),
        [jax.ShapeDtypeStruct((rows, n_dp * part), bf16)],
        [pltpu.VMEM((n_dp, rows, part), f32), pltpu.VMEM((n_dp, rows, part), bf16)]
        + add_up_scratch("ctx", [(n_dp, rows, part)])
        + dma_sems(n_dp)
        + [pltpu.SemaphoreType.DMA],
    )[0]


def attend_kernel(group, sets, rows, chunk, first_free, at_ref, q_ref, k_ref, v_ref, m_ref, o_ref, acc, total):
    step = pl.program_id(0)
    wide_head = group * HD

    @pl.when(step == 0)
    def _():
        acc[...] = jnp.zeros_like(acc)
        total[...] = jnp.zeros_like(total)

    over_width = (((1,), (1,)), ((), ()))
    of_head = lax.broadcasted_iota(jnp.int32, (8 * group, wide_head), 0) // 8
    in_head = lax.broadcasted_iota(jnp.int32, (8 * group, wide_head), 1) // HD
    ones = jnp.where(of_head == in_head, 1.0, 0.0).astype(bf16)

    def add_chunk(masked):
        is_first = m_ref[...] == 0
        for one in range(sets):
            cut = slice(one * wide_head, (one + 1) * wide_head)
            keys = k_ref[:, cut]
            both = lax.dot_general(q_ref[one], keys, over_width, preferred_element_type=f32)
            wide = keys.astype(f32)
            squares = lax.dot_general(
                ones, (wide * wide).astype(bf16), over_width, preferred_element_type=f32
            )
            inverse = lax.rsqrt(squares * (1.0 / HD) + epsilon)
            parts = []
            for h in range(group):
                at = 2 * h * rows
                scores = jnp.where(is_first, both[at : at + rows], both[at + rows : at + 2 * rows])
                probs = jnp.exp(scores * inverse[8 * h : 8 * h + 1])
                if masked:
                    key_pos = step * chunk + lax.broadcasted_iota(jnp.int32, (rows, chunk), 1)
                    row_pos = lax.broadcasted_iota(jnp.int32, (rows, chunk), 0)
                    probs = jnp.where(key_pos <= first_free + at_ref[1] + row_pos, probs, 0.0)
                total[one * group + h] += jnp.sum(probs, axis=1, keepdims=True)
                parts.append(probs.astype(bf16))
            acc[one] += jnp.dot(
                jnp.concatenate(parts, axis=0), v_ref[:, cut], preferred_element_type=f32
            )

    has_free = (step + 1) * chunk > first_free

    @pl.when(has_free)
    def _():
        add_chunk(True)

    @pl.when(jnp.logical_not(has_free))
    def _():
        add_chunk(False)

    @pl.when(step == pl.num_programs(0) - 1)
    def _():
        for head in range(sets * group):
            one, h = head // group, head % group
            summed = acc[one, h * rows : (h + 1) * rows, h * HD : (h + 1) * HD]
            o_ref[:, head * HD : (head + 1) * HD] = (summed / total[head]).astype(bf16)


def attend(queries, key_cache, value_cache, key_modality, column, row_start, slab_len):
    heads, double, _ = queries.shape
    rows = double // 2
    cache_len = key_cache.shape[0]
    chunk = min(1024, cache_len)
    width = heads * HD
    group = 2 if heads % 2 == 0 else 1
    sets = heads // group
    apart = jnp.eye(group, dtype=bf16)[None, :, None, :, None]
    queries = queries.reshape(sets, group, double, 1, HD) * apart
    queries = queries.reshape(sets, group * double, group * HD)
    where_at = jnp.stack([column, row_start]).astype(jnp.int32)
    return pl.pallas_call(
        functools.partial(attend_kernel, group, sets, rows, chunk, cache_len - slab_len),
        out_shape=jax.ShapeDtypeStruct((rows, width), bf16),
        grid_spec=pltpu.PrefetchScalarGridSpec(
            num_scalar_prefetch=1,
            grid=(cache_len // chunk,),
            in_specs=[
                pl.BlockSpec((sets, group * double, group * HD), lambda j, at: (0, 0, 0)),
                pl.BlockSpec((chunk, width), lambda j, at: (j, at[0])),
                pl.BlockSpec((chunk, width), lambda j, at: (j, at[0])),
                pl.BlockSpec((1, chunk), lambda j, at: (0, j)),
            ],
            out_specs=pl.BlockSpec((rows, width), lambda j, at: (0, 0)),
            scratch_shapes=[
                pltpu.VMEM((sets, group * rows, group * HD), f32),
                pltpu.VMEM((heads, rows, 1), f32),
            ],
        ),
        compiler_params=pltpu.CompilerParams(dimension_semantics=("arbitrary",)),
        name="attend",
    )(where_at, queries, key_cache, value_cache, key_modality)


def two_parts(values):
    high = values.astype(bf16)
    return high, (values - high.astype(f32)).astype(bf16)


def beside(values, columns):
    extra = jnp.stack([c.astype(bf16) for c in columns], axis=-1)
    pad = [(0, 0)] * (extra.ndim - 1) + [(0, LANES - extra.shape[-1])]
    return jnp.concatenate([values.astype(bf16), jnp.pad(extra, pad)], axis=-1)


def per_device(
    hidden_in,
    query_modality,
    key_cache,
    value_cache,
    key_modality,
    norm_attn,
    query_weight,
    query_gain,
    key_gain,
    out_weight,
    norm_ffn,
    gate_weight,
    up_weight,
    down_weight,
):
    m = lax.axis_index("mod")
    d = lax.axis_index("dp")
    n_mod, n_ctx, n_dp = lax.axis_size("mod"), lax.axis_size("ctx"), lax.axis_size("dp")
    rows, model = hidden_in.shape[1:]
    part = model // n_dp
    width = query_weight.shape[2]
    hidden_units = gate_weight.shape[2]
    heads = width // HD
    slab_len = n_mod * n_ctx * rows
    by_heads = heads % n_mod == 0

    hidden = hidden_in[0]
    wide = hidden.astype(f32)
    inverse = lax.rsqrt(jnp.mean(wide * wide, axis=-1) + epsilon)
    sent = jnp.broadcast_to(
        beside(jnp.zeros((rows, 0), bf16), (query_modality[0], *two_parts(inverse)))[None],
        (n_dp, rows, LANES),
    )
    pieces = hidden.reshape(rows, n_dp, part).transpose(1, 0, 2)
    own_block, slab = enter(jnp.concatenate([pieces, sent], axis=-1), 0)
    tags = slab[..., part : part + 3].astype(f32)
    ids = tags[..., 0]
    is_mine = ids == m.astype(f32)

    gain = lax.dynamic_slice_in_dim(norm_attn[0], d * part, part)
    row_inverse = (tags[..., 1] + tags[..., 2])[..., None]
    normed = jnp.where(
        is_mine[..., None], slab[..., :part].astype(f32) * row_inverse * gain, 0.0
    ).astype(bf16)
    tokens = n_dp * slab_len
    projected = jnp.dot(
        normed.reshape(tokens, part), query_weight[0], preferred_element_type=f32
    ).astype(bf16)
    gains = jnp.stack(two_parts(query_gain[0]))
    gains = jnp.where(jnp.arange(n_mod)[:, None, None] == m, gains[None], jnp.zeros_like(gains)[None])
    gains = jnp.pad(gains.reshape(2 * n_mod, width), ((0, 16 - 2 * n_mod), (0, 0)))
    gains = jnp.where(d == 0, gains, jnp.zeros_like(gains))
    split_width = width // n_mod if by_heads else width
    blocks = n_ctx * n_mod if by_heads else n_ctx
    count = blocks * rows
    if by_heads:
        to_sum = jnp.concatenate(
            [
                projected.reshape(n_dp, count, width),
                jnp.broadcast_to(gains[None], (n_dp, 16, width)),
            ],
            axis=1,
        )
        to_sum = to_sum.reshape(n_dp, count + 16, n_mod, split_width).transpose(0, 2, 1, 3)
    else:
        to_sum = jnp.concatenate(
            [
                projected.reshape(n_dp, n_mod, count, width),
                jnp.broadcast_to(gains[None, None], (n_dp, n_mod, 16, width)),
            ],
            axis=2,
        )
    (summed,) = reduce(
        (to_sum,), "dp", lambda ref, j, i: ref.at[i, j], [(count + 16, split_width)], 1
    )
    projected = summed[:count]
    both_gains = summed[count : count + 2 * n_mod : 2] + summed[count + 1 : count + 2 * n_mod : 2]
    split_heads = split_width // HD
    own_ids = lax.dynamic_index_in_dim(ids, d, 0, keepdims=False)
    if by_heads:
        own_ids = own_ids.reshape(count)
        column, row_start = m, jnp.int32(0)
        key_gains = lax.dynamic_slice_in_dim(key_gain, m * split_width, split_width, 1)
    else:
        own_ids = lax.dynamic_index_in_dim(own_ids, m, 0, keepdims=False).reshape(count)
        column, row_start = jnp.int32(0), m * count
        key_gains = key_gain
    token_gain = jnp.where(own_ids[:, None] == 0, both_gains[0][None], both_gains[1][None])
    by_head = projected.reshape(count, split_heads, HD)
    by_head = by_head * lax.rsqrt(
        jnp.mean(by_head * by_head, axis=-1, keepdims=True) + epsilon
    )
    by_head = by_head * token_gain.reshape(count, split_heads, HD) * (1.0 / math.sqrt(HD))
    queries = by_head[None] * key_gains.reshape(2, 1, split_heads, HD)
    queries = (
        queries.astype(bf16).transpose(2, 0, 1, 3).reshape(split_heads, 2 * count, HD)
    )
    head_out = attend(
        queries, key_cache[0], value_cache[0], key_modality, column, row_start, slab_len
    )

    if by_heads:
        shared = gather(
            head_out,
            "dp",
            (n_dp, count, width),
            lambda ref, j, i: ref.at[i, :, pl.ds(pl.multiple_of(j * split_width, LANES), split_width)],
            2,
        )
    else:
        shared = gather(
            head_out, "dp", (n_dp, n_mod, count, width), lambda ref, j, i: ref.at[i, j], 2
        )

    def own_product(values, weight):
        values = values.reshape(tokens, values.shape[-1])
        product = jnp.dot(values, weight, preferred_element_type=f32)
        product = jnp.where(is_mine.reshape(tokens, 1), product, 0.0).astype(bf16)
        return product.reshape(n_dp, n_mod, n_ctx, rows, part)

    residual, slab = renew(own_product(shared, out_weight[0]), own_block, 3)

    gain = lax.dynamic_slice_in_dim(norm_ffn[0], d * part, part)
    scaled = jnp.where(is_mine[..., None], slab[..., :part].astype(f32) * gain, 0.0)
    scaled = scaled.astype(bf16).reshape(tokens, part)
    by_block = (n_dp, n_mod, n_ctx * rows)
    gate, up = expand(scaled, gate_weight[0].T, up_weight[0].T)
    squares = jnp.where(is_mine[..., None], slab[..., part:], jnp.zeros_like(slab[..., part:]))
    shared = activate(
        gate.reshape(*by_block, hidden_units),
        up.reshape(*by_block, hidden_units),
        squares.reshape(*by_block, LANES),
        model,
        5,
    )
    return leave(own_product(shared, down_weight[0]), residual, 7)[None]


def solution(mesh):
    placed = (
        P("dp", ("mod", "ctx"), None),
        P("dp", ("mod", "ctx")),
        P("dp", None, "ctx"),
        P("dp", None, "ctx"),
        P("dp", None),
        P("mod", None),
        P("mod", "dp", "ctx"),
        P("mod", "ctx"),
        P(None, "ctx"),
        P("mod", "ctx", "dp"),
        P("mod", None),
        P("mod", "dp", "ctx"),
        P("mod", "dp", "ctx"),
        P("mod", "ctx", "dp"),
    )
    return jax.shard_map(
        per_device,
        mesh=mesh,
        in_specs=placed,
        out_specs=P("dp", ("mod", "ctx"), None),
        check_vma=False,
    )
```
